128 devices in a mesh: dp: 4 (over y), sp: 32 (over z, x, core).
Axes of the slice: x: 4, y: 4, z: 4, core: 2. Of those that a mesh axis runs over, the one named last changes fastest.
Arguments:
- query_matrix: bfloat16 [4, 16384, 8192], P('dp', 'sp'), may hold values from -8 to 8
- key_matrix: bfloat16 [4, 16384, 1024], P('dp', 'sp'), may hold values from -8 to 8
- value_matrix: bfloat16 [4, 16384, 1024], P('dp', 'sp'), may hold values from -6 to 6
- block_source: int32 [32, 16], replicated, may hold values from 0 to 15, as said below
- documents: int32 [4, 128], P('dp'), may hold values from 0 to 31, never falling along the last dimension, each value on 1 to 8 neighbouring positions
Outputs:
- attended: bfloat16 [4, 16384, 8192], P('dp', 'sp')
The draws below stay inside these ranges and needn't reach their ends.
Inputs may be any that keep to these rules, and one draw needn't show every extreme that they name: `block_source`: each row is a permutation of 0 to 15, and for every pair of dp indices g and h exactly 1 entries of row s at positions g * 4 to g * 4 + 3 lie in h * 4 to h * 4 + 3. `documents`: each row never falls, and a document spans at most 8 blocks.
All inputs are finite; a program needn't handle non-finite values.
Results may differ from the reference program's by a relative error of at most 0.0036.
Values may be sent and summed in bfloat16 or wider, within the bound.
A program may use at most 128 MiB of HBM per device.

```python
import math
import jax
import jax.numpy as jnp
import numpy as np
from jax import lax

QUERY_HEADS = 64
KEY_VALUE_HEADS = 8
HEAD_WIDTH = 128
BALANCE_TOKENS = 128
MOST_BLK = 8
CAP = 1
BLK_DEV = 4
GROUP_TOKENS = 16384
GB = 128
N_DP = 4
N_SP = 32


def base_values(key, width):
    return jnp.clip(jax.random.normal(key, (N_DP, GROUP_TOKENS, width), jnp.float32), -6.0, 6.0)


def draw_key_matrix(key, part):
    field_values = base_values(jax.random.fold_in(key, 1), KEY_VALUE_HEADS * HEAD_WIDTH)
    return field_values.astype(jnp.bfloat16)


def draw_query_matrix(key, part):
    field_values = base_values(jax.random.fold_in(key, 2), QUERY_HEADS * HEAD_WIDTH)
    return field_values.astype(jnp.bfloat16)


def draw_block_source(key, part):

    def one_column(column_key):
        slot_key, dest_key, place_key = jax.random.split(column_key, 3)
        slot_order = jax.vmap(lambda sub: jax.random.permutation(sub, BLK_DEV))(jax.random.split(slot_key, N_DP))
        dest_order = jax.vmap(lambda sub: jax.random.permutation(sub, N_DP))(jax.random.split(dest_key, N_DP))
        sources = jnp.arange(N_DP, dtype=jnp.int32)[:, None] * BLK_DEV + slot_order.astype(jnp.int32)
        pieces = sources.reshape(N_DP, N_DP, CAP)
        piece_of = jnp.argsort(dest_order, axis=1, stable=True)
        picker = jnp.broadcast_to(piece_of[:, :, None], (N_DP, N_DP, CAP))
        incoming = jnp.take_along_axis(pieces, picker, axis=1)
        incoming = jnp.transpose(incoming, (1, 0, 2)).reshape(N_DP, BLK_DEV)
        placing = jax.vmap(lambda sub: jax.random.permutation(sub, BLK_DEV))(jax.random.split(place_key, N_DP))
        return jnp.take_along_axis(incoming, placing, axis=1).reshape(-1)
    return jax.vmap(one_column)(jax.random.split(key, N_SP)).astype(jnp.int32)


def level_of(stream_key, dims, shards, smallest, top_value):
    def one(dim, blocks):
        draws = jax.random.uniform(jax.random.fold_in(jax.random.fold_in(stream_key, 6), dim), (blocks,), jnp.float32, smallest / len(shards), top_value / len(shards))
        return jnp.repeat(jnp.exp(draws), dims[dim] // blocks).reshape((-1,) + (1,) * (len(dims) - dim - 1))

    loudness = one(*shards[0])
    for cut in shards[1:]:
        loudness = loudness * one(*cut)
    return loudness


def length_profile(amount, total, bound, slope):
    loads = [(1 << 20) // math.isqrt(standing ** slope) + 1 for standing in range(2, amount + 1)]
    rest, holding = total - bound - (amount - 1), [1] * (amount - 1)
    while rest > 0:
        candidates = [i for i in range(amount - 1) if holding[i] < bound]
        mass, remaining = sum([loads[i] for i in candidates]), rest
        for i in candidates:
            addition = min(bound - holding[i], max(1, remaining * loads[i] // mass), rest)
            holding[i] = holding[i] + addition
            rest = rest - addition
    return np.array([bound] + holding)


def uneven(own_key, number_of, total, limit, slope):
    if number_of == 2:
        one = jax.random.randint(own_key, (), max(1, total - limit), min(limit, total - 1) + 1)
        return jnp.stack([one, total - one])
    lengths = jnp.asarray(length_profile(number_of, total, limit, slope), jnp.int32)
    twos = (number_of - 1) // 2
    giver, sink = lengths[1:1 + 2 * twos:2], lengths[2:2 + 2 * twos:2]
    slack = jnp.minimum(giver - 1, limit - sink)
    shifted = jax.random.randint(jax.random.fold_in(own_key, 1), (twos,), 0, 1 << 20) % (slack + 1)
    lengths = lengths.at[1:1 + 2 * twos:2].set(giver - shifted).at[2:2 + 2 * twos:2].set(sink + shifted)
    return lengths[jax.random.permutation(jax.random.fold_in(own_key, 2), number_of)]


def noise(key, shape, spread, reach, cuts=(), kind=jnp.bfloat16):
    drawn = jax.random.normal(key, shape, jnp.float32) * spread
    if len(cuts) > 0:
        drawn = level_of(key, shape, cuts, -0.22, 0.18) * drawn
    return jnp.clip(drawn, min=-reach, max=reach).astype(kind)


def setup_inputs(seed: int = 0) -> dict:
    streams_of = jax.random.split(jax.random.key(seed), 6)
    return {
        "query_matrix": draw_query_matrix(jax.random.fold_in(streams_of[5], 71), 0),
        "key_matrix": draw_key_matrix(jax.random.fold_in(streams_of[5], 71), 0),
        "value_matrix": noise(streams_of[2], (N_DP, GROUP_TOKENS, KEY_VALUE_HEADS * HEAD_WIDTH), 1.0, 6.0, ((0, 4), (1, 32))),
        "block_source": draw_block_source(jax.random.fold_in(streams_of[5], 71), 0),
        "documents": jax.vmap(lambda own: jnp.searchsorted(jnp.cumsum(uneven(own, GB // 4, GB, MOST_BLK, 2)), jnp.arange(GB), side="right"))(jax.random.split(streams_of[4], N_DP)).reshape((N_DP, GB)).astype(jnp.int32),
    }


def even_out_blocks(field_values, sender_group, sender_position, column_number):
    width = field_values.shape[-1]
    reshaped_rows = field_values.reshape(N_DP, N_SP, BLK_DEV, BALANCE_TOKENS, width)
    return reshaped_rows[sender_group, column_number, sender_position].reshape(N_DP, GROUP_TOKENS, width)


def attend_group(query_group, key_group, value_group, block_docs):
    span = MOST_BLK * BALANCE_TOKENS
    key_padded = jnp.pad(key_group, ((0, span), (0, 0)))
    value_padded = jnp.pad(value_group, ((0, span), (0, 0)))
    token_docs = jnp.pad(jnp.repeat(block_docs, BALANCE_TOKENS), (0, span), constant_values=-1)
    doc_first = jnp.sum(block_docs[None, :] < block_docs[:, None], axis=1, dtype=jnp.int32) * BALANCE_TOKENS
    scale = HEAD_WIDTH ** -0.5

    def one_block(block_number):
        start = block_number * BALANCE_TOKENS
        query_tile = lax.dynamic_slice_in_dim(query_group, start, BALANCE_TOKENS, 0).astype(jnp.float32)
        first = doc_first[block_number]
        key_tile = lax.dynamic_slice_in_dim(key_padded, first, span, 0).astype(jnp.float32)
        value_tile = lax.dynamic_slice_in_dim(value_padded, first, span, 0).astype(jnp.float32)
        key_docs = lax.dynamic_slice_in_dim(token_docs, first, span, 0)
        key_pos = first + jnp.arange(span, dtype=jnp.int32)
        query_pos = start + jnp.arange(BALANCE_TOKENS, dtype=jnp.int32)
        allowed = (key_docs[None, :] == block_docs[block_number]) & (key_pos[None, :] <= query_pos[:, None])
        scores = jnp.einsum("qhd,kd->qhk", query_tile, key_tile) * scale
        scores = jnp.where(allowed[:, None, :], scores, -1e30)
        top = jnp.max(scores, axis=-1, keepdims=True)
        weights = jnp.where(allowed[:, None, :], jnp.exp(scores - top), 0.0)
        total = jnp.sum(weights, axis=-1, keepdims=True)
        rounded = lax.optimization_barrier(weights.astype(jnp.bfloat16)).astype(jnp.float32)
        mixed = jnp.einsum("qhk,kd->qhd", rounded, value_tile) / total
        return mixed.astype(jnp.bfloat16)

    blocks_out = lax.map(one_block, jnp.arange(GB, dtype=jnp.int32))
    return blocks_out.reshape(GROUP_TOKENS, query_group.shape[1], HEAD_WIDTH)


def reference(query_matrix, key_matrix, value_matrix, block_source, documents):
    routing = block_source.reshape(N_SP, N_DP, BLK_DEV)
    sender_group = jnp.transpose(routing // BLK_DEV, (1, 0, 2))
    sender_position = jnp.transpose(routing % BLK_DEV, (1, 0, 2))
    column_number = jnp.broadcast_to(jnp.arange(N_SP, dtype=jnp.int32)[None, :, None], sender_group.shape)
    group_length = QUERY_HEADS // KEY_VALUE_HEADS
    query_list = even_out_blocks(query_matrix, sender_group, sender_position, column_number).reshape(N_DP, GROUP_TOKENS, KEY_VALUE_HEADS, group_length, HEAD_WIDTH)
    every_key = even_out_blocks(key_matrix, sender_group, sender_position, column_number).reshape(N_DP, GROUP_TOKENS, KEY_VALUE_HEADS, HEAD_WIDTH)
    every_value = even_out_blocks(value_matrix, sender_group, sender_position, column_number).reshape(N_DP, GROUP_TOKENS, KEY_VALUE_HEADS, HEAD_WIDTH)
    query_entries = jnp.transpose(query_list, (0, 2, 1, 3, 4)).reshape(N_DP * KEY_VALUE_HEADS, GROUP_TOKENS, group_length, HEAD_WIDTH)
    key_entries = jnp.transpose(every_key, (0, 2, 1, 3)).reshape(N_DP * KEY_VALUE_HEADS, GROUP_TOKENS, HEAD_WIDTH)
    value_entries = jnp.transpose(every_value, (0, 2, 1, 3)).reshape(N_DP * KEY_VALUE_HEADS, GROUP_TOKENS, HEAD_WIDTH)
    document_items = jnp.repeat(documents, KEY_VALUE_HEADS, axis=0)
    output_rows = lax.map(lambda item: attend_group(item[0], item[1], item[2], item[3]),
                      (query_entries, key_entries, value_entries, document_items))
    output_rows = output_rows.reshape(N_DP, KEY_VALUE_HEADS, GROUP_TOKENS, group_length, HEAD_WIDTH)
    return jnp.transpose(output_rows, (0, 2, 1, 3, 4)).reshape(N_DP, GROUP_TOKENS, QUERY_HEADS * HEAD_WIDTH)
```

```python
import jax
import jax.numpy as jnp
from jax import lax
from jax.experimental import pallas as pl
from jax.experimental.pallas import tpu as pltpu
from jax.sharding import PartitionSpec as P

QUERY_HEADS = 64
KEY_VALUE_HEADS = 8
HEAD_WIDTH = 128
BALANCE_TOKENS = 128
MOST_BLK = 8
BLK_DEV = 4
N_DP = 4
N_SP = 32
GROUP = QUERY_HEADS // KEY_VALUE_HEADS
CHUNKS = KEY_VALUE_HEADS
CHUNK_WIDTH = GROUP * HEAD_WIDTH
HALO = MOST_BLK - 1
WINDOW = HALO + BLK_DEV
SPAN = MOST_BLK * BALANCE_TOKENS
MASKED = -1e30
LOG2E = 1.4426950408889634
MESH = pl.DeviceIdType.MESH


def fused_kernel(
    source_ref,
    docs_ref,
    q_hbm,
    k_hbm,
    v_hbm,
    out_hbm,
    q_local,
    k_local,
    v_local,
    q_send,
    q_recv,
    kv_send,
    kv_recv,
    window,
    q_slots,
    bias,
    staged,
    load_sem,
    q_send_sem,
    q_recv_sem,
    kv_send_sem,
    kv_recv_sem,
    halo_send_sem,
    halo_recv_sem,
    store_sem,
):
    g = lax.axis_index("dp")
    s = lax.axis_index("sp")

    def dp_peer(step):
        return (lax.rem(g + step, N_DP), s)

    def sp_peer(step):
        return (g, lax.rem(s + step + N_SP, N_SP))

    k_load = pltpu.make_async_copy(k_hbm, k_local, load_sem.at[0])
    v_load = pltpu.make_async_copy(v_hbm, v_local, load_sem.at[1])

    def q_load(c):
        columns = pl.ds(pl.multiple_of(c * CHUNK_WIDTH, CHUNK_WIDTH), CHUNK_WIDTH)
        return pltpu.make_async_copy(q_hbm.at[:, :, columns], q_local.at[c], load_sem.at[2 + c])

    k_load.start()
    v_load.start()

    @pl.loop(0, CHUNKS)
    def _(c):
        q_load(c).start()

    barrier = pltpu.get_barrier_semaphore()
    for step in range(1, N_DP):
        pl.semaphore_signal(barrier, 1, device_id=dp_peer(step), device_id_type=MESH)
    for step in (1, 2, -1, -2):
        pl.semaphore_signal(barrier, 1, device_id=sp_peer(step), device_id_type=MESH)

    def departing(step):
        dest = lax.rem(g + step, N_DP)
        chosen = 0
        for slot in range(BLK_DEV):
            entry = source_ref[s, dest * BLK_DEV + slot]
            chosen = chosen + jnp.where((entry >> 2) == g, entry & 3, 0)
        return chosen

    def arrived_from(slot):
        entry = source_ref[s, g * BLK_DEV + slot]
        return (g - (entry >> 2)) & 3

    leaves = [departing(step) for step in range(N_DP)]
    comes = [arrived_from(slot) for slot in range(BLK_DEV)]

    for slot in range(BLK_DEV):
        own = docs_ref[s * BLK_DEV + slot]
        for j in range(HALO):
            block = s * BLK_DEV + slot + j - HALO
            same = (docs_ref[jnp.maximum(block, 0)] == own) & (block >= 0)
            level = jnp.where(same, 0.0, MASKED).astype(jnp.float32)
            bias[slot, :, pl.ds(j * BALANCE_TOKENS, BALANCE_TOKENS)] = jnp.full(
                (8, BALANCE_TOKENS), level, jnp.float32
            )

    def kv_copy(step):
        return pltpu.make_async_remote_copy(
            src_ref=kv_send.at[step - 1],
            dst_ref=kv_recv.at[step],
            send_sem=kv_send_sem.at[step - 1],
            recv_sem=kv_recv_sem.at[step - 1],
            device_id=dp_peer(step),
            device_id_type=MESH,
        )

    def q_copy(c, step):
        return pltpu.make_async_remote_copy(
            src_ref=q_send.at[c, step - 1],
            dst_ref=q_recv.at[c, step],
            send_sem=q_send_sem.at[c, step - 1],
            recv_sem=q_recv_sem.at[c, step - 1],
            device_id=dp_peer(step),
            device_id_type=MESH,
        )

    def near_copy(c):
        return pltpu.make_async_remote_copy(
            src_ref=window.at[c, pl.ds(HALO, BLK_DEV)],
            dst_ref=window.at[c, pl.ds(HALO - BLK_DEV, BLK_DEV)],
            send_sem=halo_send_sem.at[c, 0],
            recv_sem=halo_recv_sem.at[c, 0],
            device_id=sp_peer(1),
            device_id_type=MESH,
        )

    def far_copy(c):
        return pltpu.make_async_remote_copy(
            src_ref=window.at[c, pl.ds(WINDOW - (HALO - BLK_DEV), HALO - BLK_DEV)],
            dst_ref=window.at[c, pl.ds(0, HALO - BLK_DEV)],
            send_sem=halo_send_sem.at[c, 1],
            recv_sem=halo_recv_sem.at[c, 1],
            device_id=sp_peer(2),
            device_id_type=MESH,
        )

    k_load.wait()
    v_load.wait()
    for step in range(N_DP):
        target = kv_recv.at[0] if step == 0 else kv_send.at[step - 1]
        for c in range(CHUNKS):
            columns = pl.ds(c * HEAD_WIDTH, HEAD_WIDTH)
            target[c, 0] = k_local[leaves[step], :, columns]
            target[c, 1] = v_local[leaves[step], :, columns]

    pl.semaphore_wait(barrier, 7)
    for step in range(1, N_DP):
        kv_copy(step).start()

    @pl.loop(0, CHUNKS)
    def _(c):
        q_load(c).wait()

    @pl.loop(0, CHUNKS)
    def _(c):
        for step in range(1, N_DP):
            q_send[c, step - 1] = q_local[c, leaves[step]]
            q_copy(c, step).start()
        q_recv[c, 0] = q_local[c, leaves[0]]

    for step in range(1, N_DP):
        kv_copy(step).wait_recv()
    for slot in range(BLK_DEV):
        for c in range(CHUNKS):
            window[c, HALO + slot] = kv_recv[comes[slot], c]

    @pl.loop(0, CHUNKS)
    def _(c):
        near_copy(c).start()
        far_copy(c).start()

    row = lax.broadcasted_iota(jnp.int32, (BALANCE_TOKENS, BALANCE_TOKENS), 0)
    column = lax.broadcasted_iota(jnp.int32, (BALANCE_TOKENS, BALANCE_TOKENS), 1)
    triangle = jnp.where(column <= row, 0.0, MASKED).astype(jnp.float32)
    diagonal = jnp.concatenate([triangle, triangle], axis=0)
    factor = LOG2E * HEAD_WIDTH ** -0.5

    def store_copy(c):
        columns = pl.ds(pl.multiple_of(c * CHUNK_WIDTH, CHUNK_WIDTH), CHUNK_WIDTH)
        return pltpu.make_async_copy(
            staged.at[lax.rem(c, 2)], out_hbm.at[:, :, columns], store_sem.at[lax.rem(c, 2)]
        )

    @pl.loop(0, CHUNKS)
    def _(c):
        near_copy(c).wait_recv()
        far_copy(c).wait_recv()
        for step in range(1, N_DP):
            q_copy(c, step).wait_recv()

        @pl.when(c >= 2)
        def _():
            store_copy(c - 2).wait()

        for slot in range(BLK_DEV):
            for head in range(GROUP):
                columns = pl.ds(head * HEAD_WIDTH, HEAD_WIDTH)
                chosen = q_recv[c, 0, :, columns]
                for step in range(1, N_DP):
                    chosen = jnp.where(comes[slot] == step, q_recv[c, step, :, columns], chosen)
                q_slots[slot, pl.ds(head * BALANCE_TOKENS, BALANCE_TOKENS)] = chosen

        side = lax.rem(c, 2)

        @pl.loop(0, BLK_DEV)
        def _(slot):
            keys = window[c, pl.ds(slot, MOST_BLK), 0].reshape(SPAN, HEAD_WIDTH)
            values = window[c, pl.ds(slot, MOST_BLK), 1].reshape(SPAN, HEAD_WIDTH)
            level = bias[slot, pl.ds(0, 1)]
            for pair in range(GROUP // 2):
                queries = q_slots[slot, pl.ds(pair * 2 * BALANCE_TOKENS, 2 * BALANCE_TOKENS)]
                scores = lax.dot_general(
                    queries, keys, (((1,), (1,)), ((), ())), preferred_element_type=jnp.float32
                )
                far = scores[:, : HALO * BALANCE_TOKENS] + level
                near = scores[:, HALO * BALANCE_TOKENS :] + diagonal
                scores = jnp.concatenate([far, near], axis=1)
                top = jnp.max(scores, axis=1, keepdims=True)
                weights = jnp.exp2((scores - top) * factor)
                total = jnp.sum(weights, axis=1, keepdims=True)
                mixed = jnp.dot(
                    weights.astype(jnp.bfloat16), values, preferred_element_type=jnp.float32
                )
                result = (mixed / total).astype(jnp.bfloat16)
                for part in range(2):
                    staged[
                        side, slot, :, pl.ds((2 * pair + part) * HEAD_WIDTH, HEAD_WIDTH)
                    ] = result[part * BALANCE_TOKENS : (part + 1) * BALANCE_TOKENS]

        store_copy(c).start()

    store_copy(CHUNKS - 2).wait()
    store_copy(CHUNKS - 1).wait()
    for step in range(1, N_DP):
        kv_copy(step).wait_send()

    @pl.loop(0, CHUNKS)
    def _(c):
        near_copy(c).wait_send()
        far_copy(c).wait_send()
        for step in range(1, N_DP):
            q_copy(c, step).wait_send()


def on_device(query_matrix, key_matrix, value_matrix, block_source, documents):
    bf16 = jnp.bfloat16
    tokens = BALANCE_TOKENS
    blocks = (BLK_DEV, tokens)
    dma = pltpu.SemaphoreType.DMA
    kv_width = KEY_VALUE_HEADS * HEAD_WIDTH
    width = QUERY_HEADS * HEAD_WIDTH
    smem = pl.BlockSpec(memory_space=pltpu.SMEM)
    anywhere = pl.BlockSpec(memory_space=pl.ANY)
    attended = pl.pallas_call(
        fused_kernel,
        out_shape=jax.ShapeDtypeStruct((*blocks, width), bf16),
        in_specs=[smem, smem, anywhere, anywhere, anywhere],
        out_specs=anywhere,
        scratch_shapes=[
            pltpu.VMEM((CHUNKS, *blocks, CHUNK_WIDTH), bf16),
            pltpu.VMEM((*blocks, kv_width), bf16),
            pltpu.VMEM((*blocks, kv_width), bf16),
            pltpu.VMEM((CHUNKS, N_DP - 1, tokens, CHUNK_WIDTH), bf16),
            pltpu.VMEM((CHUNKS, N_DP, tokens, CHUNK_WIDTH), bf16),
            pltpu.VMEM((N_DP - 1, CHUNKS, 2, tokens, HEAD_WIDTH), bf16),
            pltpu.VMEM((N_DP, CHUNKS, 2, tokens, HEAD_WIDTH), bf16),
            pltpu.VMEM((CHUNKS, WINDOW, 2, tokens, HEAD_WIDTH), bf16),
            pltpu.VMEM((BLK_DEV, GROUP * tokens, HEAD_WIDTH), bf16),
            pltpu.VMEM((BLK_DEV, 8, HALO * tokens), jnp.float32),
            pltpu.VMEM((2, *blocks, CHUNK_WIDTH), bf16),
            dma((2 + CHUNKS,)),
            dma((CHUNKS, N_DP - 1)),
            dma((CHUNKS, N_DP - 1)),
            dma((N_DP - 1,)),
            dma((N_DP - 1,)),
            dma((CHUNKS, 2)),
            dma((CHUNKS, 2)),
            dma((2,)),
        ],
        compiler_params=pltpu.CompilerParams(
            collective_id=0, has_side_effects=True, vmem_limit_bytes=60 << 20
        ),
        name="balanced_attention",
    )(
        block_source,
        documents.reshape(-1),
        query_matrix.reshape(*blocks, width),
        key_matrix.reshape(*blocks, kv_width),
        value_matrix.reshape(*blocks, kv_width),
    )
    return attended.reshape(1, BLK_DEV * tokens, width)


def solution(mesh):
    placed = (P("dp", "sp", None), P("dp", "sp", None), P("dp", "sp", None), P(), P("dp", None))
    return jax.shard_map(
        on_device, mesh=mesh, in_specs=placed, out_specs=P("dp", "sp", None), check_vma=False
    )
```

```python
import jax
import jax.numpy as jnp
from jax import lax
from jax.experimental import pallas as pl
from jax.experimental.pallas import tpu as pltpu
from jax.sharding import PartitionSpec as P

QUERY_HEADS = 64
KEY_VALUE_HEADS = 8
HEAD_WIDTH = 128
BALANCE_TOKENS = 128
MOST_BLK = 8
BLK_DEV = 4
N_DP = 4
N_SP = 32
GROUP = QUERY_HEADS // KEY_VALUE_HEADS
PART = 2
PARTS = QUERY_HEADS // PART
PART_WIDTH = PART * HEAD_WIDTH
PER_KV = GROUP // PART
HALO = MOST_BLK - 1
WINDOW = HALO + BLK_DEV
SPAN = MOST_BLK * BALANCE_TOKENS
MASKED = -1e30
LOG2E = 1.4426950408889634
MESH = pl.DeviceIdType.MESH


def fused_kernel(
    source_hbm,
    docs_ref,
    q_hbm,
    k_hbm,
    v_hbm,
    out_ref,
    source_ref,
    q_local,
    k_local,
    v_local,
    q_send,
    q_recv,
    kv_send,
    kv_recv,
    window,
    bias,
    load_sem,
    q_load_sem,
    q_send_sem,
    q_recv_sem,
    kv_send_sem,
    kv_recv_sem,
    halo_send_sem,
    halo_recv_sem,
):
    g = lax.axis_index("dp")
    s = lax.axis_index("sp")

    def dp_peer(step):
        return (lax.rem(g + step, N_DP), s)

    def sp_peer(step):
        return (g, lax.rem(s + step + N_SP, N_SP))

    source_load = pltpu.make_async_copy(source_hbm, source_ref, load_sem.at[0])
    k_load = pltpu.make_async_copy(k_hbm, k_local, load_sem.at[1])
    v_load = pltpu.make_async_copy(v_hbm, v_local, load_sem.at[2])
    source_load.start()
    k_load.start()
    v_load.start()

    def q_load(c):
        columns = pl.ds(c * GROUP * HEAD_WIDTH, GROUP * HEAD_WIDTH)
        return pltpu.make_async_copy(
            q_hbm.at[:, :, columns], q_local.at[:, :, columns], q_load_sem.at[c]
        )

    barrier = pltpu.get_barrier_semaphore()
    for step in range(1, N_DP):
        pl.semaphore_signal(barrier, 1, device_id=dp_peer(step), device_id_type=MESH)
    for step in (1, 2, -1, -2):
        pl.semaphore_signal(barrier, 1, device_id=sp_peer(step), device_id_type=MESH)

    source_load.wait()

    def departing(step):
        dest = lax.rem(g + step, N_DP)
        chosen = 0
        for slot in range(BLK_DEV):
            entry = source_ref[dest * BLK_DEV + slot, s]
            chosen = chosen + jnp.where((entry >> 2) == g, entry & 3, 0)
        return chosen

    def arrived_from(slot):
        entry = source_ref[g * BLK_DEV + slot, s]
        return (g - (entry >> 2)) & 3

    leaves = [departing(step) for step in range(N_DP)]
    comes = [arrived_from(slot) for slot in range(BLK_DEV)]

    def kv_copy(step):
        return pltpu.make_async_remote_copy(
            src_ref=kv_send.at[step - 1],
            dst_ref=kv_recv.at[step],
            send_sem=kv_send_sem.at[step - 1],
            recv_sem=kv_recv_sem.at[step - 1],
            device_id=dp_peer(step),
            device_id_type=MESH,
        )

    def q_copy(part, step):
        return pltpu.make_async_remote_copy(
            src_ref=q_send.at[part, step - 1],
            dst_ref=q_recv.at[part, step],
            send_sem=q_send_sem.at[part, step - 1],
            recv_sem=q_recv_sem.at[part, step - 1],
            device_id=dp_peer(step),
            device_id_type=MESH,
        )

    def near_copy(c):
        return pltpu.make_async_remote_copy(
            src_ref=window.at[c, pl.ds(HALO, BLK_DEV)],
            dst_ref=window.at[c, pl.ds(HALO - BLK_DEV, BLK_DEV)],
            send_sem=halo_send_sem.at[c, 0],
            recv_sem=halo_recv_sem.at[c, 0],
            device_id=sp_peer(1),
            device_id_type=MESH,
        )

    def far_copy(c):
        return pltpu.make_async_remote_copy(
            src_ref=window.at[c, pl.ds(WINDOW - (HALO - BLK_DEV), HALO - BLK_DEV)],
            dst_ref=window.at[c, pl.ds(0, HALO - BLK_DEV)],
            send_sem=halo_send_sem.at[c, 1],
            recv_sem=halo_recv_sem.at[c, 1],
            device_id=sp_peer(2),
            device_id_type=MESH,
        )

    k_load.wait()
    v_load.wait()
    for c in range(KEY_VALUE_HEADS):
        q_load(c).start()
    for step in (2, 1, 3, 0):
        target = kv_recv.at[0] if step == 0 else kv_send.at[step - 1]
        for c in range(KEY_VALUE_HEADS):
            columns = pl.ds(c * HEAD_WIDTH, HEAD_WIDTH)
            target[c, 0] = k_local[leaves[step], :, columns]
            target[c, 1] = v_local[leaves[step], :, columns]
        if step == 2:
            pl.semaphore_wait(barrier, 7)
        if step > 0:
            kv_copy(step).start()

    for c in range(KEY_VALUE_HEADS):
        q_load(c).wait()

    @pl.loop(0, PARTS)
    def _(part):
        columns = pl.ds(pl.multiple_of(part * PART_WIDTH, PART_WIDTH), PART_WIDTH)
        for step in (2, 1, 3):
            q_send[part, step - 1] = q_local[leaves[step], :, columns]
            q_copy(part, step).start()
        q_recv[part, 0] = q_local[leaves[0], :, columns]

    for slot in range(BLK_DEV):
        own = docs_ref[s * BLK_DEV + slot]
        for j in range(HALO):
            block = s * BLK_DEV + slot + j - HALO
            same = (docs_ref[jnp.maximum(block, 0)] == own) & (block >= 0)
            level = jnp.where(same, 0.0, MASKED).astype(jnp.float32)
            bias[slot, :, pl.ds(j * BALANCE_TOKENS, BALANCE_TOKENS)] = jnp.full(
                (8, BALANCE_TOKENS), level, jnp.float32
            )

    for step in range(1, N_DP):
        kv_copy(step).wait_recv()
    for slot in range(BLK_DEV):
        for c in range(KEY_VALUE_HEADS):
            window[c, HALO + slot] = kv_recv[comes[slot], c]

    @pl.loop(0, KEY_VALUE_HEADS)
    def _(c):
        near_copy(c).start()
        far_copy(c).start()

    row = lax.broadcasted_iota(jnp.int32, (BALANCE_TOKENS, BALANCE_TOKENS), 0)
    column = lax.broadcasted_iota(jnp.int32, (BALANCE_TOKENS, BALANCE_TOKENS), 1)
    triangle = jnp.where(column <= row, 0.0, MASKED).astype(jnp.float32)
    diagonal = jnp.concatenate([triangle] * PART, axis=0)
    factor = LOG2E * HEAD_WIDTH ** -0.5

    @pl.loop(0, PARTS)
    def _(part):
        c = part // PER_KV

        @pl.when(lax.rem(part, PER_KV) == 0)
        def _():
            near_copy(c).wait_recv()
            far_copy(c).wait_recv()

        for step in range(1, N_DP):
            q_copy(part, step).wait_recv()

        for slot in range(BLK_DEV):
            arrived = q_recv[part, 0]
            for step in range(1, N_DP):
                arrived = jnp.where(comes[slot] == step, q_recv[part, step], arrived)
            queries = jnp.concatenate(
                [arrived[:, h * HEAD_WIDTH : (h + 1) * HEAD_WIDTH] for h in range(PART)], axis=0
            )
            keys = window[c, pl.ds(slot, MOST_BLK), 0].reshape(SPAN, HEAD_WIDTH)
            values = window[c, pl.ds(slot, MOST_BLK), 1].reshape(SPAN, HEAD_WIDTH)
            level = bias[slot, pl.ds(0, 1)]
            scores = lax.dot_general(
                queries, keys, (((1,), (1,)), ((), ())), preferred_element_type=jnp.float32
            )
            far = scores[:, : HALO * BALANCE_TOKENS] + level
            near = scores[:, HALO * BALANCE_TOKENS :] + diagonal
            scores = jnp.concatenate([far, near], axis=1)
            top = jnp.max(scores, axis=1, keepdims=True)
            weights = jnp.exp2((scores - top) * factor)
            total = jnp.sum(weights, axis=1, keepdims=True)
            mixed = jnp.dot(
                weights.astype(jnp.bfloat16), values, preferred_element_type=jnp.float32
            )
            result = (mixed / total).astype(jnp.bfloat16)
            columns = pl.ds(pl.multiple_of(part * PART_WIDTH, PART_WIDTH), PART_WIDTH)
            out_ref[slot, :, columns] = jnp.concatenate(
                [result[h * BALANCE_TOKENS : (h + 1) * BALANCE_TOKENS] for h in range(PART)], axis=1
            )

    for step in range(1, N_DP):
        kv_copy(step).wait_send()

    @pl.loop(0, KEY_VALUE_HEADS)
    def _(c):
        near_copy(c).wait_send()
        far_copy(c).wait_send()

    @pl.loop(0, PARTS)
    def _(part):
        for step in range(1, N_DP):
            q_copy(part, step).wait_send()


def on_device(query_matrix, key_matrix, value_matrix, block_source, documents):
    bf16 = jnp.bfloat16
    tokens = BALANCE_TOKENS
    blocks = (BLK_DEV, tokens)
    dma = pltpu.SemaphoreType.DMA
    kv_width = KEY_VALUE_HEADS * HEAD_WIDTH
    width = QUERY_HEADS * HEAD_WIDTH
    smem = pl.BlockSpec(memory_space=pltpu.SMEM)
    anywhere = pl.BlockSpec(memory_space=pl.ANY)
    attended = pl.pallas_call(
        fused_kernel,
        out_shape=pltpu.VMEM((*blocks, width), bf16),
        in_specs=[anywhere, smem, anywhere, anywhere, anywhere],
        out_specs=pl.BlockSpec(memory_space=pltpu.VMEM),
        scratch_shapes=[
            pltpu.SMEM(block_source.shape[::-1], jnp.int32),
            pltpu.VMEM((*blocks, width), bf16),
            pltpu.VMEM((*blocks, kv_width), bf16),
            pltpu.VMEM((*blocks, kv_width), bf16),
            pltpu.VMEM((PARTS, N_DP - 1, tokens, PART_WIDTH), bf16),
            pltpu.VMEM((PARTS, N_DP, tokens, PART_WIDTH), bf16),
            pltpu.VMEM((N_DP - 1, KEY_VALUE_HEADS, 2, tokens, HEAD_WIDTH), bf16),
            pltpu.VMEM((N_DP, KEY_VALUE_HEADS, 2, tokens, HEAD_WIDTH), bf16),
            pltpu.VMEM((KEY_VALUE_HEADS, WINDOW, 2, tokens, HEAD_WIDTH), bf16),
            pltpu.VMEM((BLK_DEV, 8, HALO * tokens), jnp.float32),
            dma((3,)),
            dma((KEY_VALUE_HEADS,)),
            dma((PARTS, N_DP - 1)),
            dma((PARTS, N_DP - 1)),
            dma((N_DP - 1,)),
            dma((N_DP - 1,)),
            dma((KEY_VALUE_HEADS, 2)),
            dma((KEY_VALUE_HEADS, 2)),
        ],
        compiler_params=pltpu.CompilerParams(
            collective_id=0, has_side_effects=True, vmem_limit_bytes=48 << 20
        ),
        name="balanced_attention",
    )(
        block_source.T,
        documents.reshape(-1),
        query_matrix.reshape(*blocks, width),
        key_matrix.reshape(*blocks, kv_width),
        value_matrix.reshape(*blocks, kv_width),
    )
    return attended.reshape(1, BLK_DEV * tokens, width)


def solution(mesh):
    placed = (P("dp", "sp", None), P("dp", "sp", None), P("dp", "sp", None), P(), P("dp", None))
    return jax.shard_map(
        on_device, mesh=mesh, in_specs=placed, out_specs=P("dp", "sp", None), check_vma=False
    )
```

```python
import jax
import jax.numpy as jnp
from jax import lax
from jax.experimental import pallas as pl
from jax.experimental.pallas import tpu as pltpu
from jax.sharding import PartitionSpec as P

QUERY_HEADS = 64
KEY_VALUE_HEADS = 8
HEAD_WIDTH = 128
BALANCE_TOKENS = 128
MOST_BLK = 8
BLK_DEV = 4
N_DP = 4
N_SP = 32
GROUP = QUERY_HEADS // KEY_VALUE_HEADS
PART = 2
PARTS = QUERY_HEADS // PART
PART_WIDTH = PART * HEAD_WIDTH
PER_KV = GROUP // PART
PIECES = 4
PIECE_HEADS = KEY_VALUE_HEADS // PIECES
PIECE_WIDTH = PIECE_HEADS * HEAD_WIDTH
HALO = MOST_BLK - 1
WINDOW = HALO + BLK_DEV
SPAN = MOST_BLK * BALANCE_TOKENS
MASKED = -1e30
LOG2E = 1.4426950408889634
MESH = pl.DeviceIdType.MESH


def fused_kernel(
    source_hbm,
    docs_ref,
    q_hbm,
    k_hbm,
    v_hbm,
    out_ref,
    source_ref,
    q_local,
    k_local,
    v_local,
    q_send,
    q_recv,
    kv_send,
    kv_recv,
    window,
    bias,
    load_sem,
    q_load_sem,
    q_send_sem,
    q_recv_sem,
    kv_send_sem,
    kv_recv_sem,
    halo_send_sem,
    halo_recv_sem,
    ready,
):
    g = lax.axis_index("dp")
    s = lax.axis_index("sp")

    def dp_peer(step):
        return (lax.rem(g + step, N_DP), s)

    def sp_peer(step):
        return (g, lax.rem(s + step, N_SP))

    source_load = pltpu.make_async_copy(source_hbm, source_ref, load_sem.at[0])

    def kv_load(kind, piece):
        columns = pl.ds(piece * PIECE_WIDTH, PIECE_WIDTH)
        return pltpu.make_async_copy(
            (k_hbm, v_hbm)[kind].at[:, :, columns],
            (k_local, v_local)[kind][piece],
            load_sem.at[1 + 2 * piece + kind],
        )

    source_load.start()
    for piece in range(PIECES):
        kv_load(0, piece).start()
        kv_load(1, piece).start()

    def q_load(c):
        columns = pl.ds(c * GROUP * HEAD_WIDTH, GROUP * HEAD_WIDTH)
        return pltpu.make_async_copy(
            q_hbm.at[:, :, columns], q_local.at[:, :, columns], q_load_sem.at[c]
        )

    barrier = pltpu.get_barrier_semaphore()
    for step in range(1, N_DP):
        pl.semaphore_signal(barrier, 1, device_id=dp_peer(step), device_id_type=MESH)

    def greet(semaphore, column):
        pl.semaphore_signal(semaphore, 1, device_id=(g, column), device_id_type=MESH)

    @pl.when((s == 1) | (s >= 3))
    def _():
        greet(barrier, s - 1)

    @pl.when(s >= 4)
    def _():
        greet(barrier, s - 2)

    def enter():
        @pl.when(s == 0)
        def _():
            pl.semaphore_wait(barrier, 4)
            greet(barrier, 2)

        @pl.when(s == 1)
        def _():
            pl.semaphore_wait(barrier, 3)
            greet(barrier, 2)
            greet(barrier, 3)

        @pl.when(s == 2)
        def _():
            pl.semaphore_wait(barrier, 7)
            greet(ready, 0)
            greet(ready, 1)

        @pl.when(s == 3)
        def _():
            pl.semaphore_wait(barrier, 6)
            greet(ready, 1)

        @pl.when((s >= 4) & (s <= N_SP - 3))
        def _():
            pl.semaphore_wait(barrier, 5)

        @pl.when(s == N_SP - 2)
        def _():
            pl.semaphore_wait(barrier, 4)

        @pl.when(s == N_SP - 1)
        def _():
            pl.semaphore_wait(barrier, 3)

    source_load.wait()

    def departing(step):
        dest = lax.rem(g + step, N_DP)
        chosen = 0
        for slot in range(BLK_DEV):
            entry = source_ref[dest * BLK_DEV + slot, s]
            chosen = chosen + jnp.where((entry >> 2) == g, entry & 3, 0)
        return chosen

    def arrived_from(slot):
        entry = source_ref[g * BLK_DEV + slot, s]
        return (g - (entry >> 2)) & 3

    leaves = [departing(step) for step in range(N_DP)]
    comes = [arrived_from(slot) for slot in range(BLK_DEV)]

    def turns(turn, number):
        if turn >= 2:
            step = (2, 0)[turn - 2]
            return step, leaves[step]
        step = 1 + 2 * lax.rem(s + number + turn, 2)
        return step, jnp.where(step == 1, leaves[1], leaves[3])

    def kv_copy(piece, step):
        heads = pl.ds(piece * PIECE_HEADS, PIECE_HEADS)
        return pltpu.make_async_remote_copy(
            src_ref=kv_send.at[step - 1, heads],
            dst_ref=kv_recv.at[step, heads],
            send_sem=kv_send_sem.at[piece, step - 1],
            recv_sem=kv_recv_sem.at[piece, step - 1],
            device_id=dp_peer(step),
            device_id_type=MESH,
        )

    def q_copy(part, step):
        return pltpu.make_async_remote_copy(
            src_ref=q_send.at[part, step - 1],
            dst_ref=q_recv.at[part, step],
            send_sem=q_send_sem.at[part, step - 1],
            recv_sem=q_recv_sem.at[part, step - 1],
            device_id=dp_peer(step),
            device_id_type=MESH,
        )

    def near_copy(c):
        return pltpu.make_async_remote_copy(
            src_ref=window.at[c, pl.ds(HALO, BLK_DEV)],
            dst_ref=window.at[c, pl.ds(HALO - BLK_DEV, BLK_DEV)],
            send_sem=halo_send_sem.at[c, 0],
            recv_sem=halo_recv_sem.at[c, 0],
            device_id=sp_peer(1),
            device_id_type=MESH,
        )

    def far_copy(c):
        return pltpu.make_async_remote_copy(
            src_ref=window.at[c, pl.ds(WINDOW - (HALO - BLK_DEV), HALO - BLK_DEV)],
            dst_ref=window.at[c, pl.ds(0, HALO - BLK_DEV)],
            send_sem=halo_send_sem.at[c, 1],
            recv_sem=halo_recv_sem.at[c, 1],
            device_id=sp_peer(2),
            device_id_type=MESH,
        )

    for piece in range(PIECES):
        kv_load(0, piece).wait()
        kv_load(1, piece).wait()
        if piece == PIECES - 1:
            for c in range(KEY_VALUE_HEADS):
                q_load(c).start()
        for turn in range(N_DP):
            step, leaf = turns(turn, piece)
            for head in range(PIECE_HEADS):
                columns = pl.ds(head * HEAD_WIDTH, HEAD_WIDTH)
                key = k_local[piece][leaf, :, columns]
                value = v_local[piece][leaf, :, columns]
                if turn < N_DP - 1:
                    kv_send[step - 1, piece * PIECE_HEADS + head, 0] = key
                    kv_send[step - 1, piece * PIECE_HEADS + head, 1] = value
                else:
                    kv_recv[0, piece * PIECE_HEADS + head, 0] = key
                    kv_recv[0, piece * PIECE_HEADS + head, 1] = value
            if piece == 0 and turn == 0:
                enter()
            if turn < N_DP - 1:
                kv_copy(piece, step).start()

    for c in range(KEY_VALUE_HEADS):
        q_load(c).wait()

    @pl.loop(0, PARTS)
    def _(part):
        columns = pl.ds(pl.multiple_of(part * PART_WIDTH, PART_WIDTH), PART_WIDTH)
        for turn in range(N_DP - 1):
            step, leaf = turns(turn, part)
            q_send[part, step - 1] = q_local[leaf, :, columns]
            q_copy(part, step).start()
        q_recv[part, 0] = q_local[leaves[0], :, columns]

    for slot in range(BLK_DEV):
        own = docs_ref[s * BLK_DEV + slot]
        for j in range(HALO):
            block = s * BLK_DEV + slot + j - HALO
            same = (docs_ref[jnp.maximum(block, 0)] == own) & (block >= 0)
            level = jnp.where(same, 0.0, MASKED).astype(jnp.float32)
            bias[slot, :, pl.ds(j * BALANCE_TOKENS, BALANCE_TOKENS)] = jnp.full(
                (8, BALANCE_TOKENS), level, jnp.float32
            )

    for piece in range(PIECES):
        for step in range(1, N_DP):
            kv_copy(piece, step).wait_recv()
    for slot in range(BLK_DEV):
        for c in range(KEY_VALUE_HEADS):
            window[c, HALO + slot] = kv_recv[comes[slot], c]

    def each_halo(near_act, far_act, near_when, far_when):
        @pl.when(near_when)
        def _():
            @pl.loop(0, KEY_VALUE_HEADS)
            def _(c):
                near_act(c)

                @pl.when(far_when)
                def _():
                    far_act(c)

    @pl.when(s == 0)
    def _():
        pl.semaphore_wait(ready, 1)

    @pl.when(s == 1)
    def _():
        pl.semaphore_wait(ready, 2)

    each_halo(
        lambda c: near_copy(c).start(),
        lambda c: far_copy(c).start(),
        s < N_SP - 1,
        s < N_SP - 2,
    )

    @pl.when(s < 2)
    def _():
        @pl.loop(0, KEY_VALUE_HEADS)
        def _(c):
            window[c, pl.ds(0, HALO - BLK_DEV)] = jnp.zeros(
                (HALO - BLK_DEV, 2, BALANCE_TOKENS, HEAD_WIDTH), jnp.bfloat16
            )

    @pl.when(s < 1)
    def _():
        @pl.loop(0, KEY_VALUE_HEADS)
        def _(c):
            window[c, pl.ds(HALO - BLK_DEV, BLK_DEV)] = jnp.zeros(
                (BLK_DEV, 2, BALANCE_TOKENS, HEAD_WIDTH), jnp.bfloat16
            )

    row = lax.broadcasted_iota(jnp.int32, (BALANCE_TOKENS, BALANCE_TOKENS), 0)
    column = lax.broadcasted_iota(jnp.int32, (BALANCE_TOKENS, BALANCE_TOKENS), 1)
    triangle = jnp.where(column <= row, 0.0, MASKED).astype(jnp.float32)
    diagonal = jnp.concatenate([triangle] * PART, axis=0)
    factor = LOG2E * HEAD_WIDTH ** -0.5

    @pl.loop(0, PARTS)
    def _(part):
        c = part // PER_KV

        @pl.when((lax.rem(part, PER_KV) == 0) & (s >= 1))
        def _():
            near_copy(c).wait_recv()

        @pl.when((lax.rem(part, PER_KV) == 0) & (s >= 2))
        def _():
            far_copy(c).wait_recv()

        for step in range(1, N_DP):
            q_copy(part, step).wait_recv()

        for slot in range(BLK_DEV):
            arrived = q_recv[part, 0]
            for step in range(1, N_DP):
                arrived = jnp.where(comes[slot] == step, q_recv[part, step], arrived)
            queries = jnp.concatenate(
                [arrived[:, h * HEAD_WIDTH : (h + 1) * HEAD_WIDTH] for h in range(PART)], axis=0
            )
            keys = window[c, pl.ds(slot, MOST_BLK), 0].reshape(SPAN, HEAD_WIDTH)
            values = window[c, pl.ds(slot, MOST_BLK), 1].reshape(SPAN, HEAD_WIDTH)
            widened = jnp.concatenate([values, jnp.ones_like(values)], axis=1)
            level = bias[slot, pl.ds(0, 1)]
            scores = lax.dot_general(
                queries, keys, (((1,), (1,)), ((), ())), preferred_element_type=jnp.float32
            )
            far = scores[:, : HALO * BALANCE_TOKENS] + level
            near = scores[:, HALO * BALANCE_TOKENS :] + diagonal
            scores = jnp.concatenate([far, near], axis=1)
            top = jnp.max(scores, axis=1, keepdims=True)
            weights = jnp.exp2((scores - top) * factor)
            mixed = jnp.dot(
                weights.astype(jnp.bfloat16), widened, preferred_element_type=jnp.float32
            )
            result = (mixed[:, :HEAD_WIDTH] / mixed[:, HEAD_WIDTH:]).astype(jnp.bfloat16)
            columns = pl.ds(pl.multiple_of(part * PART_WIDTH, PART_WIDTH), PART_WIDTH)
            out_ref[slot, :, columns] = jnp.concatenate(
                [result[h * BALANCE_TOKENS : (h + 1) * BALANCE_TOKENS] for h in range(PART)], axis=1
            )

    for piece in range(PIECES):
        for step in range(1, N_DP):
            kv_copy(piece, step).wait_send()

    each_halo(
        lambda c: near_copy(c).wait_send(),
        lambda c: far_copy(c).wait_send(),
        s < N_SP - 1,
        s < N_SP - 2,
    )

    @pl.loop(0, PARTS)
    def _(part):
        for step in range(1, N_DP):
            q_copy(part, step).wait_send()


def on_device(query_matrix, key_matrix, value_matrix, block_source, documents):
    bf16 = jnp.bfloat16
    tokens = BALANCE_TOKENS
    blocks = (BLK_DEV, tokens)
    dma = pltpu.SemaphoreType.DMA
    kv_width = KEY_VALUE_HEADS * HEAD_WIDTH
    width = QUERY_HEADS * HEAD_WIDTH
    smem = pl.BlockSpec(memory_space=pltpu.SMEM)
    anywhere = pl.BlockSpec(memory_space=pl.ANY)
    attended = pl.pallas_call(
        fused_kernel,
        out_shape=pltpu.VMEM((*blocks, width), bf16),
        in_specs=[anywhere, smem, anywhere, anywhere, anywhere],
        out_specs=pl.BlockSpec(memory_space=pltpu.VMEM),
        scratch_shapes=[
            pltpu.SMEM(block_source.shape[::-1], jnp.int32),
            pltpu.VMEM((*blocks, width), bf16),
            [pltpu.VMEM((*blocks, PIECE_WIDTH), bf16)] * PIECES,
            [pltpu.VMEM((*blocks, PIECE_WIDTH), bf16)] * PIECES,
            pltpu.VMEM((PARTS, N_DP - 1, tokens, PART_WIDTH), bf16),
            pltpu.VMEM((PARTS, N_DP, tokens, PART_WIDTH), bf16),
            pltpu.VMEM((N_DP - 1, KEY_VALUE_HEADS, 2, tokens, HEAD_WIDTH), bf16),
            pltpu.VMEM((N_DP, KEY_VALUE_HEADS, 2, tokens, HEAD_WIDTH), bf16),
            pltpu.VMEM((KEY_VALUE_HEADS, WINDOW, 2, tokens, HEAD_WIDTH), bf16),
            pltpu.VMEM((BLK_DEV, 8, HALO * tokens), jnp.float32),
            dma((1 + 2 * PIECES,)),
            dma((KEY_VALUE_HEADS,)),
            dma((PARTS, N_DP - 1)),
            dma((PARTS, N_DP - 1)),
            dma((PIECES, N_DP - 1)),
            dma((PIECES, N_DP - 1)),
            dma((KEY_VALUE_HEADS, 2)),
            dma((KEY_VALUE_HEADS, 2)),
            pltpu.SemaphoreType.REGULAR,
        ],
        compiler_params=pltpu.CompilerParams(
            collective_id=0, has_side_effects=True, vmem_limit_bytes=48 << 20
        ),
        name="balanced_attention",
    )(
        block_source.T,
        documents.reshape(-1),
        query_matrix.reshape(*blocks, width),
        key_matrix.reshape(*blocks, kv_width),
        value_matrix.reshape(*blocks, kv_width),
    )
    return attended.reshape(1, BLK_DEV * tokens, width)


def solution(mesh):
    placed = (P("dp", "sp", None), P("dp", "sp", None), P("dp", "sp", None), P(), P("dp", None))
    return jax.shard_map(
        on_device, mesh=mesh, in_specs=placed, out_specs=P("dp", "sp", None), check_vma=False
    )
```

```python
import jax
import jax.numpy as jnp
from jax import lax
from jax.experimental import pallas as pl
from jax.experimental.pallas import tpu as pltpu
from jax.sharding import PartitionSpec as P

QUERY_HEADS = 64
KEY_VALUE_HEADS = 8
HEAD_WIDTH = 128
BALANCE_TOKENS = 128
MOST_BLK = 8
BLK_DEV = 4
N_DP = 4
N_SP = 32
GROUP = QUERY_HEADS // KEY_VALUE_HEADS
PAIR = 2
WHOLE = KEY_VALUE_HEADS - 2
HALF = GROUP // 2
LAST = KEY_VALUE_HEADS - 1
PAIRS = GROUP // PAIR - 1
SINGLES = 2
GROUPS = WHOLE + 2 + PAIRS + SINGLES
PIECES = 2
PIECE_HEADS = KEY_VALUE_HEADS // PIECES
PIECE_WIDTH = PIECE_HEADS * HEAD_WIDTH
HALO = MOST_BLK - 1
WINDOW = HALO + BLK_DEV
SPAN = MOST_BLK * BALANCE_TOKENS
MASKED = -1e30
LOG2E = 1.4426950408889634
MESH = pl.DeviceIdType.MESH


def fused_kernel(
    source_hbm,
    docs_ref,
    q_hbm,
    k_hbm,
    v_hbm,
    out_ref,
    source_ref,
    q_local,
    k_local,
    v_local,
    q_send,
    q_recv,
    kv_send,
    kv_recv,
    window,
    bias,
    load_sem,
    q_load_sem,
    q_send_sem,
    q_recv_sem,
    kv_send_sem,
    kv_recv_sem,
    halo_send_sem,
    halo_recv_sem,
    ready,
):
    g = lax.axis_index("dp")
    s = lax.axis_index("sp")

    def dp_peer(step):
        return (lax.rem(g + step, N_DP), s)

    def sp_peer(step):
        return (g, lax.rem(s + step, N_SP))

    source_load = pltpu.make_async_copy(source_hbm, source_ref, load_sem.at[0])

    def kv_load(kind, piece):
        columns = pl.ds(piece * PIECE_WIDTH, PIECE_WIDTH)
        return pltpu.make_async_copy(
            (k_hbm, v_hbm)[kind].at[:, :, columns],
            (k_local, v_local)[kind][piece],
            load_sem.at[1 + 2 * piece + kind],
        )

    source_load.start()
    for piece in range(PIECES):
        kv_load(0, piece).start()
        kv_load(1, piece).start()

    def q_load(c):
        columns = pl.ds(c * GROUP * HEAD_WIDTH, GROUP * HEAD_WIDTH)
        return pltpu.make_async_copy(
            q_hbm.at[:, :, columns], q_local.at[:, :, columns], q_load_sem.at[c]
        )

    barrier = pltpu.get_barrier_semaphore()
    for step in range(1, N_DP):
        pl.semaphore_signal(barrier, 1, device_id=dp_peer(step), device_id_type=MESH)

    def greet(semaphore, column):
        pl.semaphore_signal(semaphore, 1, device_id=(g, column), device_id_type=MESH)

    @pl.when((s == 1) | (s >= 3))
    def _():
        greet(barrier, s - 1)

    @pl.when(s >= 4)
    def _():
        greet(barrier, s - 2)

    def enter():
        @pl.when(s == 0)
        def _():
            pl.semaphore_wait(barrier, 4)
            greet(barrier, 2)

        @pl.when(s == 1)
        def _():
            pl.semaphore_wait(barrier, 3)
            greet(barrier, 2)
            greet(barrier, 3)

        @pl.when(s == 2)
        def _():
            pl.semaphore_wait(barrier, 7)
            greet(ready, 0)
            greet(ready, 1)

        @pl.when(s == 3)
        def _():
            pl.semaphore_wait(barrier, 6)
            greet(ready, 1)

        @pl.when((s >= 4) & (s <= N_SP - 3))
        def _():
            pl.semaphore_wait(barrier, 5)

        @pl.when(s == N_SP - 2)
        def _():
            pl.semaphore_wait(barrier, 4)

        @pl.when(s == N_SP - 1)
        def _():
            pl.semaphore_wait(barrier, 3)

    source_load.wait()

    def departing(step):
        dest = lax.rem(g + step, N_DP)
        chosen = 0
        for slot in range(BLK_DEV):
            entry = source_ref[dest * BLK_DEV + slot, s]
            chosen = chosen + jnp.where((entry >> 2) == g, entry & 3, 0)
        return chosen

    def arrived_from(slot):
        entry = source_ref[g * BLK_DEV + slot, s]
        return (g - (entry >> 2)) & 3

    leaves = [departing(step) for step in range(N_DP)]
    comes = [arrived_from(slot) for slot in range(BLK_DEV)]

    def turns(turn, number):
        if turn >= 2:
            step = (2, 0)[turn - 2]
            return step, leaves[step]
        step = 1 + 2 * lax.rem(s + number + turn, 2)
        return step, jnp.where(step == 1, leaves[1], leaves[3])

    def kv_copy(piece, step):
        heads = pl.ds(piece * PIECE_HEADS, PIECE_HEADS)
        return pltpu.make_async_remote_copy(
            src_ref=kv_send.at[step - 1, heads],
            dst_ref=kv_recv.at[step, heads],
            send_sem=kv_send_sem.at[piece, step - 1],
            recv_sem=kv_recv_sem.at[piece, step - 1],
            device_id=dp_peer(step),
            device_id_type=MESH,
        )

    def q_copy(group, first, count, step):
        heads = pl.ds(first, count)
        return pltpu.make_async_remote_copy(
            src_ref=q_send.at[step - 1, heads],
            dst_ref=q_recv.at[step, heads],
            send_sem=q_send_sem.at[group, step - 1],
            recv_sem=q_recv_sem.at[group, step - 1],
            device_id=dp_peer(step),
            device_id_type=MESH,
        )

    def each_group(act):
        @pl.loop(0, WHOLE)
        def _(c):
            act(c, c * GROUP, GROUP)

        @pl.loop(0, 2)
        def _(i):
            act(WHOLE + i, WHOLE * GROUP + i * HALF, HALF)

        @pl.loop(0, PAIRS)
        def _(i):
            act(WHOLE + 2 + i, LAST * GROUP + i * PAIR, PAIR)

        @pl.loop(0, SINGLES)
        def _(i):
            act(GROUPS - SINGLES + i, QUERY_HEADS - SINGLES + i, 1)

    def near_copy(c):
        return pltpu.make_async_remote_copy(
            src_ref=window.at[c, pl.ds(HALO, BLK_DEV)],
            dst_ref=window.at[c, pl.ds(HALO - BLK_DEV, BLK_DEV)],
            send_sem=halo_send_sem.at[c, 0],
            recv_sem=halo_recv_sem.at[c, 0],
            device_id=sp_peer(1),
            device_id_type=MESH,
        )

    def far_copy(c):
        return pltpu.make_async_remote_copy(
            src_ref=window.at[c, pl.ds(WINDOW - (HALO - BLK_DEV), HALO - BLK_DEV)],
            dst_ref=window.at[c, pl.ds(0, HALO - BLK_DEV)],
            send_sem=halo_send_sem.at[c, 1],
            recv_sem=halo_recv_sem.at[c, 1],
            device_id=sp_peer(2),
            device_id_type=MESH,
        )

    for piece in range(PIECES):
        kv_load(0, piece).wait()
        kv_load(1, piece).wait()
        if piece == PIECES - 1:
            for c in range(KEY_VALUE_HEADS):
                q_load(c).start()
        for turn in range(N_DP):
            step, leaf = turns(turn, piece)
            for head in range(PIECE_HEADS):
                columns = pl.ds(head * HEAD_WIDTH, HEAD_WIDTH)
                key = k_local[piece][leaf, :, columns]
                value = v_local[piece][leaf, :, columns]
                if turn < N_DP - 1:
                    kv_send[step - 1, piece * PIECE_HEADS + head, 0] = key
                    kv_send[step - 1, piece * PIECE_HEADS + head, 1] = value
                else:
                    kv_recv[0, piece * PIECE_HEADS + head, 0] = key
                    kv_recv[0, piece * PIECE_HEADS + head, 1] = value
            if piece == 0 and turn == 0:
                enter()
            if turn < N_DP - 1:
                kv_copy(piece, step).start()

    for c in range(KEY_VALUE_HEADS):
        q_load(c).wait()

    def send_group(group, first, count):
        for turn in range(N_DP):
            step, leaf = turns(turn, group)
            for i in range(count):
                head = first + i
                columns = pl.ds(pl.multiple_of(head * HEAD_WIDTH, HEAD_WIDTH), HEAD_WIDTH)
                block = q_local[leaf, :, columns]
                if turn < N_DP - 1:
                    q_send[step - 1, head] = block
                else:
                    q_recv[0, head] = block
            if turn < N_DP - 1:
                q_copy(group, first, count, step).start()

    each_group(send_group)

    for slot in range(BLK_DEV):
        own = docs_ref[s * BLK_DEV + slot]
        for j in range(HALO):
            block = s * BLK_DEV + slot + j - HALO
            same = (docs_ref[jnp.maximum(block, 0)] == own) & (block >= 0)
            level = jnp.where(same, 0.0, MASKED).astype(jnp.float32)
            bias[slot, :, pl.ds(j * BALANCE_TOKENS, BALANCE_TOKENS)] = jnp.full(
                (8, BALANCE_TOKENS), level, jnp.float32
            )

    for piece in range(PIECES):
        for step in range(1, N_DP):
            kv_copy(piece, step).wait_recv()
    for slot in range(BLK_DEV):
        for c in range(KEY_VALUE_HEADS):
            window[c, HALO + slot] = kv_recv[comes[slot], c]

    def each_halo(near_act, far_act, near_when, far_when):
        @pl.when(near_when)
        def _():
            @pl.loop(0, KEY_VALUE_HEADS)
            def _(c):
                near_act(c)

                @pl.when(far_when)
                def _():
                    far_act(c)

    @pl.when(s == 0)
    def _():
        pl.semaphore_wait(ready, 1)

    @pl.when(s == 1)
    def _():
        pl.semaphore_wait(ready, 2)

    each_halo(
        lambda c: near_copy(c).start(),
        lambda c: far_copy(c).start(),
        s < N_SP - 1,
        s < N_SP - 2,
    )

    @pl.when(s < 2)
    def _():
        @pl.loop(0, KEY_VALUE_HEADS)
        def _(c):
            window[c, pl.ds(0, HALO - BLK_DEV)] = jnp.zeros(
                (HALO - BLK_DEV, 2, BALANCE_TOKENS, HEAD_WIDTH), jnp.bfloat16
            )

    @pl.when(s < 1)
    def _():
        @pl.loop(0, KEY_VALUE_HEADS)
        def _(c):
            window[c, pl.ds(HALO - BLK_DEV, BLK_DEV)] = jnp.zeros(
                (BLK_DEV, 2, BALANCE_TOKENS, HEAD_WIDTH), jnp.bfloat16
            )

    row = lax.broadcasted_iota(jnp.int32, (BALANCE_TOKENS, BALANCE_TOKENS), 0)
    column = lax.broadcasted_iota(jnp.int32, (BALANCE_TOKENS, BALANCE_TOKENS), 1)
    triangle = jnp.where(column <= row, 0.0, MASKED).astype(jnp.float32)
    factor = LOG2E * HEAD_WIDTH ** -0.5

    def attend(c, first, count):
        heads = pl.ds(first, count)
        diagonal = jnp.concatenate([triangle] * count, axis=0)
        for slot in range(BLK_DEV):
            arrived = q_recv[0, heads]
            for step in range(1, N_DP):
                arrived = jnp.where(comes[slot] == step, q_recv[step, heads], arrived)
            queries = arrived.reshape(count * BALANCE_TOKENS, HEAD_WIDTH)
            keys = window[c, pl.ds(slot, MOST_BLK), 0].reshape(SPAN, HEAD_WIDTH)
            values = window[c, pl.ds(slot, MOST_BLK), 1].reshape(SPAN, HEAD_WIDTH)
            widened = jnp.concatenate([values, jnp.ones_like(values)], axis=1)
            level = bias[slot, pl.ds(0, 1)]
            scores = lax.dot_general(
                queries, keys, (((1,), (1,)), ((), ())), preferred_element_type=jnp.float32
            )
            far = scores[:, : HALO * BALANCE_TOKENS] + level
            near = scores[:, HALO * BALANCE_TOKENS :] + diagonal
            scores = jnp.concatenate([far, near], axis=1)
            top = jnp.max(scores, axis=1, keepdims=True)
            weights = jnp.exp2((scores - top) * factor)
            mixed = jnp.dot(
                weights.astype(jnp.bfloat16), widened, preferred_element_type=jnp.float32
            )
            result = (mixed[:, :HEAD_WIDTH] / mixed[:, HEAD_WIDTH:]).astype(jnp.bfloat16)
            width = count * HEAD_WIDTH
            columns = pl.ds(pl.multiple_of(first * HEAD_WIDTH, width), width)
            out_ref[slot, :, columns] = jnp.concatenate(
                [result[h * BALANCE_TOKENS : (h + 1) * BALANCE_TOKENS] for h in range(count)], axis=1
            )

    def await_group(group, first, count):
        for step in range(1, N_DP):
            q_copy(group, first, count, step).wait_recv()

    def await_halo(c):
        @pl.when(s >= 1)
        def _():
            near_copy(c).wait_recv()

        @pl.when(s >= 2)
        def _():
            far_copy(c).wait_recv()

    @pl.loop(0, WHOLE)
    def _(c):
        await_halo(c)
        await_group(c, c * GROUP, GROUP)

        @pl.loop(0, GROUP // PAIR)
        def _(i):
            attend(c, c * GROUP + i * PAIR, PAIR)

    await_halo(WHOLE)

    @pl.loop(0, 2)
    def _(i):
        await_group(WHOLE + i, WHOLE * GROUP + i * HALF, HALF)

        @pl.loop(0, HALF // PAIR)
        def _(j):
            attend(WHOLE, WHOLE * GROUP + i * HALF + j * PAIR, PAIR)

    await_halo(LAST)

    @pl.loop(0, PAIRS)
    def _(i):
        await_group(WHOLE + 2 + i, LAST * GROUP + i * PAIR, PAIR)
        attend(LAST, LAST * GROUP + i * PAIR, PAIR)

    @pl.loop(0, SINGLES)
    def _(i):
        await_group(GROUPS - SINGLES + i, QUERY_HEADS - SINGLES + i, 1)
        attend(LAST, QUERY_HEADS - SINGLES + i, 1)

    for piece in range(PIECES):
        for step in range(1, N_DP):
            kv_copy(piece, step).wait_send()

    each_halo(
        lambda c: near_copy(c).wait_send(),
        lambda c: far_copy(c).wait_send(),
        s < N_SP - 1,
        s < N_SP - 2,
    )

    def sent_group(group, first, count):
        for step in range(1, N_DP):
            q_copy(group, first, count, step).wait_send()

    each_group(sent_group)


def on_device(query_matrix, key_matrix, value_matrix, block_source, documents):
    bf16 = jnp.bfloat16
    tokens = BALANCE_TOKENS
    blocks = (BLK_DEV, tokens)
    dma = pltpu.SemaphoreType.DMA
    kv_width = KEY_VALUE_HEADS * HEAD_WIDTH
    width = QUERY_HEADS * HEAD_WIDTH
    smem = pl.BlockSpec(memory_space=pltpu.SMEM)
    anywhere = pl.BlockSpec(memory_space=pl.ANY)
    attended = pl.pallas_call(
        fused_kernel,
        out_shape=pltpu.VMEM((*blocks, width), bf16),
        in_specs=[anywhere, smem, anywhere, anywhere, anywhere],
        out_specs=pl.BlockSpec(memory_space=pltpu.VMEM),
        scratch_shapes=[
            pltpu.SMEM(block_source.shape[::-1], jnp.int32),
            pltpu.VMEM((*blocks, width), bf16),
            [pltpu.VMEM((*blocks, PIECE_WIDTH), bf16)] * PIECES,
            [pltpu.VMEM((*blocks, PIECE_WIDTH), bf16)] * PIECES,
            pltpu.VMEM((N_DP - 1, QUERY_HEADS, tokens, HEAD_WIDTH), bf16),
            pltpu.VMEM((N_DP, QUERY_HEADS, tokens, HEAD_WIDTH), bf16),
            pltpu.VMEM((N_DP - 1, KEY_VALUE_HEADS, 2, tokens, HEAD_WIDTH), bf16),
            pltpu.VMEM((N_DP, KEY_VALUE_HEADS, 2, tokens, HEAD_WIDTH), bf16),
            pltpu.VMEM((KEY_VALUE_HEADS, WINDOW, 2, tokens, HEAD_WIDTH), bf16),
            pltpu.VMEM((BLK_DEV, 8, HALO * tokens), jnp.float32),
            dma((1 + 2 * PIECES,)),
            dma((KEY_VALUE_HEADS,)),
            dma((GROUPS, N_DP - 1)),
            dma((GROUPS, N_DP - 1)),
            dma((PIECES, N_DP - 1)),
            dma((PIECES, N_DP - 1)),
            dma((KEY_VALUE_HEADS, 2)),
            dma((KEY_VALUE_HEADS, 2)),
            pltpu.SemaphoreType.REGULAR,
        ],
        compiler_params=pltpu.CompilerParams(
            collective_id=0, has_side_effects=True, vmem_limit_bytes=48 << 20
        ),
        name="balanced_attention",
    )(
        block_source.T,
        documents.reshape(-1),
        query_matrix.reshape(*blocks, width),
        key_matrix.reshape(*blocks, kv_width),
        value_matrix.reshape(*blocks, kv_width),
    )
    return attended.reshape(1, BLK_DEV * tokens, width)


def solution(mesh):
    placed = (P("dp", "sp", None), P("dp", "sp", None), P("dp", "sp", None), P(), P("dp", None))
    return jax.shard_map(
        on_device, mesh=mesh, in_specs=placed, out_specs=P("dp", "sp", None), check_vma=False
    )
```

```python
import jax
import jax.numpy as jnp
from jax import lax
from jax.experimental import pallas as pl
from jax.experimental.pallas import tpu as pltpu
from jax.sharding import PartitionSpec as P

QUERY_HEADS = 64
KEY_VALUE_HEADS = 8
HEAD_WIDTH = 128
BALANCE_TOKENS = 128
MOST_BLK = 8
BLK_DEV = 4
N_DP = 4
N_SP = 32
GROUP = QUERY_HEADS // KEY_VALUE_HEADS
PAIR = 2
WHOLE = KEY_VALUE_HEADS - 2
HALF = GROUP // 2
LAST = KEY_VALUE_HEADS - 1
PAIRS = GROUP // PAIR - 1
GROUPS = WHOLE + 2 + PAIRS + 1
TAIL = QUERY_HEADS - PAIR
TAIL_WIDTH = PAIR * HEAD_WIDTH
READY_WIDTH = TAIL * HEAD_WIDTH
PIECES = 2
PIECE_HEADS = KEY_VALUE_HEADS // PIECES
PIECE_WIDTH = PIECE_HEADS * HEAD_WIDTH
HALO = MOST_BLK - 1
WINDOW = HALO + BLK_DEV
SPAN = MOST_BLK * BALANCE_TOKENS
MASKED = -1e30
LOG2E = 1.4426950408889634
MESH = pl.DeviceIdType.MESH


def causal_levels():
    row = lax.broadcasted_iota(jnp.int32, (BALANCE_TOKENS, BALANCE_TOKENS), 0)
    column = lax.broadcasted_iota(jnp.int32, (BALANCE_TOKENS, BALANCE_TOKENS), 1)
    triangle = jnp.where(column <= row, 0.0, MASKED).astype(jnp.float32)
    return jnp.concatenate([triangle] * PAIR, axis=0)


def attend_pair(queries, keys, values, level, diagonal):
    factor = LOG2E * HEAD_WIDTH ** -0.5
    widened = jnp.concatenate([values, jnp.ones_like(values)], axis=1)
    scores = lax.dot_general(
        queries, keys, (((1,), (1,)), ((), ())), preferred_element_type=jnp.float32
    )
    far = scores[:, : HALO * BALANCE_TOKENS] + level
    near = scores[:, HALO * BALANCE_TOKENS :] + diagonal
    scores = jnp.concatenate([far, near], axis=1)
    top = jnp.max(scores, axis=1, keepdims=True)
    weights = jnp.exp2((scores - top) * factor)
    mixed = jnp.dot(weights.astype(jnp.bfloat16), widened, preferred_element_type=jnp.float32)
    result = (mixed[:, :HEAD_WIDTH] / mixed[:, HEAD_WIDTH:]).astype(jnp.bfloat16)
    return jnp.concatenate(
        [result[h * BALANCE_TOKENS : (h + 1) * BALANCE_TOKENS] for h in range(PAIR)], axis=1
    )


def finish_kernel(ready_ref, queries_ref, window_ref, bias_ref, out_hbm, staged, sem):
    copies = [
        pltpu.make_async_copy(
            ready_ref.at[slot, :, pl.ds(0, READY_WIDTH)],
            out_hbm.at[slot, :, pl.ds(0, READY_WIDTH)],
            sem.at[slot],
        )
        for slot in range(BLK_DEV)
    ]
    for copy in copies:
        copy.start()
    diagonal = causal_levels()
    for slot in range(BLK_DEV):
        staged[slot] = attend_pair(
            queries_ref[slot],
            window_ref[pl.ds(slot, MOST_BLK), 0].reshape(SPAN, HEAD_WIDTH),
            window_ref[pl.ds(slot, MOST_BLK), 1].reshape(SPAN, HEAD_WIDTH),
            bias_ref[slot, pl.ds(0, 1)],
            diagonal,
        )
    last = pltpu.make_async_copy(
        staged, out_hbm.at[:, :, pl.ds(READY_WIDTH, TAIL_WIDTH)], sem.at[BLK_DEV]
    )
    last.start()
    for copy in copies:
        copy.wait()
    last.wait()


def fused_kernel(
    source_hbm,
    docs_ref,
    q_hbm,
    k_hbm,
    v_hbm,
    out_ref,
    tail_queries,
    tail_window,
    bias,
    source_ref,
    q_local,
    k_local,
    v_local,
    q_send,
    q_recv,
    kv_send,
    kv_recv,
    window,
    load_sem,
    q_load_sem,
    q_send_sem,
    q_recv_sem,
    kv_send_sem,
    kv_recv_sem,
    halo_send_sem,
    halo_recv_sem,
    ready,
):
    g = lax.axis_index("dp")
    s = lax.axis_index("sp")

    def dp_peer(step):
        return (lax.rem(g + step, N_DP), s)

    def sp_peer(step):
        return (g, lax.rem(s + step, N_SP))

    source_load = pltpu.make_async_copy(source_hbm, source_ref, load_sem.at[0])

    def kv_load(kind, piece):
        columns = pl.ds(piece * PIECE_WIDTH, PIECE_WIDTH)
        return pltpu.make_async_copy(
            (k_hbm, v_hbm)[kind].at[:, :, columns],
            (k_local, v_local)[kind][piece],
            load_sem.at[1 + 2 * piece + kind],
        )

    source_load.start()
    for piece in range(PIECES):
        kv_load(0, piece).start()
        kv_load(1, piece).start()

    def q_load(c):
        columns = pl.ds(c * GROUP * HEAD_WIDTH, GROUP * HEAD_WIDTH)
        return pltpu.make_async_copy(
            q_hbm.at[:, :, columns], q_local.at[:, :, columns], q_load_sem.at[c]
        )

    barrier = pltpu.get_barrier_semaphore()
    for step in range(1, N_DP):
        pl.semaphore_signal(barrier, 1, device_id=dp_peer(step), device_id_type=MESH)

    def greet(semaphore, column):
        pl.semaphore_signal(semaphore, 1, device_id=(g, column), device_id_type=MESH)

    @pl.when((s == 1) | (s >= 3))
    def _():
        greet(barrier, s - 1)

    @pl.when(s >= 4)
    def _():
        greet(barrier, s - 2)

    def enter():
        @pl.when(s == 0)
        def _():
            pl.semaphore_wait(barrier, 4)
            greet(barrier, 2)

        @pl.when(s == 1)
        def _():
            pl.semaphore_wait(barrier, 3)
            greet(barrier, 2)
            greet(barrier, 3)

        @pl.when(s == 2)
        def _():
            pl.semaphore_wait(barrier, 7)
            greet(ready, 0)
            greet(ready, 1)

        @pl.when(s == 3)
        def _():
            pl.semaphore_wait(barrier, 6)
            greet(ready, 1)

        @pl.when((s >= 4) & (s <= N_SP - 3))
        def _():
            pl.semaphore_wait(barrier, 5)

        @pl.when(s == N_SP - 2)
        def _():
            pl.semaphore_wait(barrier, 4)

        @pl.when(s == N_SP - 1)
        def _():
            pl.semaphore_wait(barrier, 3)

    source_load.wait()

    def departing(step):
        dest = lax.rem(g + step, N_DP)
        chosen = 0
        for slot in range(BLK_DEV):
            entry = source_ref[dest * BLK_DEV + slot, s]
            chosen = chosen + jnp.where((entry >> 2) == g, entry & 3, 0)
        return chosen

    def arrived_from(slot):
        entry = source_ref[g * BLK_DEV + slot, s]
        return (g - (entry >> 2)) & 3

    leaves = [departing(step) for step in range(N_DP)]
    comes = [arrived_from(slot) for slot in range(BLK_DEV)]

    def turns(turn, number):
        if turn >= 2:
            step = (2, 0)[turn - 2]
            return step, leaves[step]
        step = 1 + 2 * lax.rem(s + number + turn, 2)
        return step, jnp.where(step == 1, leaves[1], leaves[3])

    def kv_copy(piece, step):
        heads = pl.ds(piece * PIECE_HEADS, PIECE_HEADS)
        return pltpu.make_async_remote_copy(
            src_ref=kv_send.at[step - 1, heads],
            dst_ref=kv_recv.at[step, heads],
            send_sem=kv_send_sem.at[piece, step - 1],
            recv_sem=kv_recv_sem.at[piece, step - 1],
            device_id=dp_peer(step),
            device_id_type=MESH,
        )

    def q_copy(group, first, count, step):
        heads = pl.ds(first, count)
        return pltpu.make_async_remote_copy(
            src_ref=q_send.at[step - 1, heads],
            dst_ref=q_recv.at[step, heads],
            send_sem=q_send_sem.at[group, step - 1],
            recv_sem=q_recv_sem.at[group, step - 1],
            device_id=dp_peer(step),
            device_id_type=MESH,
        )

    def each_group(act):
        @pl.loop(0, WHOLE)
        def _(c):
            act(c, c * GROUP, GROUP)

        @pl.loop(0, 2)
        def _(i):
            act(WHOLE + i, WHOLE * GROUP + i * HALF, HALF)

        @pl.loop(0, PAIRS + 1)
        def _(i):
            act(WHOLE + 2 + i, LAST * GROUP + i * PAIR, PAIR)


    def near_copy(c):
        return pltpu.make_async_remote_copy(
            src_ref=window.at[c, pl.ds(HALO, BLK_DEV)],
            dst_ref=window.at[c, pl.ds(HALO - BLK_DEV, BLK_DEV)],
            send_sem=halo_send_sem.at[c, 0],
            recv_sem=halo_recv_sem.at[c, 0],
            device_id=sp_peer(1),
            device_id_type=MESH,
        )

    def far_copy(c):
        return pltpu.make_async_remote_copy(
            src_ref=window.at[c, pl.ds(WINDOW - (HALO - BLK_DEV), HALO - BLK_DEV)],
            dst_ref=window.at[c, pl.ds(0, HALO - BLK_DEV)],
            send_sem=halo_send_sem.at[c, 1],
            recv_sem=halo_recv_sem.at[c, 1],
            device_id=sp_peer(2),
            device_id_type=MESH,
        )

    for piece in range(PIECES):
        kv_load(0, piece).wait()
        kv_load(1, piece).wait()
        if piece == PIECES - 1:
            for c in range(KEY_VALUE_HEADS):
                q_load(c).start()
        for turn in range(N_DP):
            step, leaf = turns(turn, piece)
            for head in range(PIECE_HEADS):
                columns = pl.ds(head * HEAD_WIDTH, HEAD_WIDTH)
                key = k_local[piece][leaf, :, columns]
                value = v_local[piece][leaf, :, columns]
                if turn < N_DP - 1:
                    kv_send[step - 1, piece * PIECE_HEADS + head, 0] = key
                    kv_send[step - 1, piece * PIECE_HEADS + head, 1] = value
                else:
                    kv_recv[0, piece * PIECE_HEADS + head, 0] = key
                    kv_recv[0, piece * PIECE_HEADS + head, 1] = value
            if piece == 0 and turn == 0:
                enter()
            if turn < N_DP - 1:
                kv_copy(piece, step).start()

    for c in range(KEY_VALUE_HEADS):
        q_load(c).wait()

    def send_group(group, first, count):
        for turn in range(N_DP):
            step, leaf = turns(turn, group)
            for i in range(count):
                head = first + i
                columns = pl.ds(pl.multiple_of(head * HEAD_WIDTH, HEAD_WIDTH), HEAD_WIDTH)
                block = q_local[leaf, :, columns]
                if turn < N_DP - 1:
                    q_send[step - 1, head] = block
                else:
                    q_recv[0, head] = block
            if turn < N_DP - 1:
                q_copy(group, first, count, step).start()

    each_group(send_group)

    for slot in range(BLK_DEV):
        own = docs_ref[s * BLK_DEV + slot]
        for j in range(HALO):
            block = s * BLK_DEV + slot + j - HALO
            same = (docs_ref[jnp.maximum(block, 0)] == own) & (block >= 0)
            level = jnp.where(same, 0.0, MASKED).astype(jnp.float32)
            bias[slot, :, pl.ds(j * BALANCE_TOKENS, BALANCE_TOKENS)] = jnp.full(
                (8, BALANCE_TOKENS), level, jnp.float32
            )

    for piece in range(PIECES):
        for step in range(1, N_DP):
            kv_copy(piece, step).wait_recv()
    for slot in range(BLK_DEV):
        for c in range(KEY_VALUE_HEADS):
            window[c, HALO + slot] = kv_recv[comes[slot], c]

    def each_halo(near_act, far_act, near_when, far_when):
        @pl.when(near_when)
        def _():
            @pl.loop(0, KEY_VALUE_HEADS)
            def _(c):
                near_act(c)

                @pl.when(far_when)
                def _():
                    far_act(c)

    @pl.when(s == 0)
    def _():
        pl.semaphore_wait(ready, 1)

    @pl.when(s == 1)
    def _():
        pl.semaphore_wait(ready, 2)

    each_halo(
        lambda c: near_copy(c).start(),
        lambda c: far_copy(c).start(),
        s < N_SP - 1,
        s < N_SP - 2,
    )

    @pl.when(s < 2)
    def _():
        @pl.loop(0, KEY_VALUE_HEADS)
        def _(c):
            window[c, pl.ds(0, HALO - BLK_DEV)] = jnp.zeros(
                (HALO - BLK_DEV, 2, BALANCE_TOKENS, HEAD_WIDTH), jnp.bfloat16
            )

    @pl.when(s < 1)
    def _():
        @pl.loop(0, KEY_VALUE_HEADS)
        def _(c):
            window[c, pl.ds(HALO - BLK_DEV, BLK_DEV)] = jnp.zeros(
                (BLK_DEV, 2, BALANCE_TOKENS, HEAD_WIDTH), jnp.bfloat16
            )

    def slot_queries(slot, first, count):
        heads = pl.ds(first, count)
        arrived = q_recv[0, heads]
        for step in range(1, N_DP):
            arrived = jnp.where(comes[slot] == step, q_recv[step, heads], arrived)
        return arrived.reshape(count * BALANCE_TOKENS, HEAD_WIDTH)

    diagonal = causal_levels()

    def attend(c, first):
        for slot in range(BLK_DEV):
            columns = pl.ds(pl.multiple_of(first * HEAD_WIDTH, TAIL_WIDTH), TAIL_WIDTH)
            out_ref[slot, :, columns] = attend_pair(
                slot_queries(slot, first, PAIR),
                window[c, pl.ds(slot, MOST_BLK), 0].reshape(SPAN, HEAD_WIDTH),
                window[c, pl.ds(slot, MOST_BLK), 1].reshape(SPAN, HEAD_WIDTH),
                bias[slot, pl.ds(0, 1)],
                diagonal,
            )

    def await_group(group, first, count):
        for step in range(1, N_DP):
            q_copy(group, first, count, step).wait_recv()

    def await_halo(c):
        @pl.when(s >= 1)
        def _():
            near_copy(c).wait_recv()

        @pl.when(s >= 2)
        def _():
            far_copy(c).wait_recv()

    @pl.loop(0, WHOLE)
    def _(c):
        await_halo(c)
        await_group(c, c * GROUP, GROUP)

        @pl.loop(0, GROUP // PAIR)
        def _(i):
            attend(c, c * GROUP + i * PAIR)

    await_halo(WHOLE)

    @pl.loop(0, 2)
    def _(i):
        await_group(WHOLE + i, WHOLE * GROUP + i * HALF, HALF)

        @pl.loop(0, HALF // PAIR)
        def _(j):
            attend(WHOLE, WHOLE * GROUP + i * HALF + j * PAIR)

    await_halo(LAST)
    tail_window[...] = window[LAST]

    @pl.loop(0, PAIRS)
    def _(i):
        await_group(WHOLE + 2 + i, LAST * GROUP + i * PAIR, PAIR)
        attend(LAST, LAST * GROUP + i * PAIR)

    await_group(GROUPS - 1, TAIL, PAIR)
    for slot in range(BLK_DEV):
        tail_queries[slot] = slot_queries(slot, TAIL, PAIR)

    for piece in range(PIECES):
        for step in range(1, N_DP):
            kv_copy(piece, step).wait_send()

    each_halo(
        lambda c: near_copy(c).wait_send(),
        lambda c: far_copy(c).wait_send(),
        s < N_SP - 1,
        s < N_SP - 2,
    )

    def sent_group(group, first, count):
        for step in range(1, N_DP):
            q_copy(group, first, count, step).wait_send()

    each_group(sent_group)


def on_device(query_matrix, key_matrix, value_matrix, block_source, documents):
    bf16 = jnp.bfloat16
    tokens = BALANCE_TOKENS
    blocks = (BLK_DEV, tokens)
    dma = pltpu.SemaphoreType.DMA
    kv_width = KEY_VALUE_HEADS * HEAD_WIDTH
    width = QUERY_HEADS * HEAD_WIDTH
    smem = pl.BlockSpec(memory_space=pltpu.SMEM)
    anywhere = pl.BlockSpec(memory_space=pl.ANY)
    vmem = pl.BlockSpec(memory_space=pltpu.VMEM)
    parts = pl.pallas_call(
        fused_kernel,
        out_shape=(
            pltpu.VMEM((*blocks, width), bf16),
            pltpu.VMEM((BLK_DEV, PAIR * tokens, HEAD_WIDTH), bf16),
            pltpu.VMEM((WINDOW, 2, tokens, HEAD_WIDTH), bf16),
            pltpu.VMEM((BLK_DEV, 8, HALO * tokens), jnp.float32),
        ),
        in_specs=[anywhere, smem, anywhere, anywhere, anywhere],
        out_specs=(vmem, vmem, vmem, vmem),
        scratch_shapes=[
            pltpu.SMEM(block_source.shape[::-1], jnp.int32),
            pltpu.VMEM((*blocks, width), bf16),
            [pltpu.VMEM((*blocks, PIECE_WIDTH), bf16)] * PIECES,
            [pltpu.VMEM((*blocks, PIECE_WIDTH), bf16)] * PIECES,
            pltpu.VMEM((N_DP - 1, QUERY_HEADS, tokens, HEAD_WIDTH), bf16),
            pltpu.VMEM((N_DP, QUERY_HEADS, tokens, HEAD_WIDTH), bf16),
            pltpu.VMEM((N_DP - 1, KEY_VALUE_HEADS, 2, tokens, HEAD_WIDTH), bf16),
            pltpu.VMEM((N_DP, KEY_VALUE_HEADS, 2, tokens, HEAD_WIDTH), bf16),
            pltpu.VMEM((KEY_VALUE_HEADS, WINDOW, 2, tokens, HEAD_WIDTH), bf16),
            dma((1 + 2 * PIECES,)),
            dma((KEY_VALUE_HEADS,)),
            dma((GROUPS, N_DP - 1)),
            dma((GROUPS, N_DP - 1)),
            dma((PIECES, N_DP - 1)),
            dma((PIECES, N_DP - 1)),
            dma((KEY_VALUE_HEADS, 2)),
            dma((KEY_VALUE_HEADS, 2)),
            pltpu.SemaphoreType.REGULAR,
        ],
        compiler_params=pltpu.CompilerParams(
            collective_id=0, has_side_effects=True, vmem_limit_bytes=48 << 20
        ),
        name="balanced_attention",
    )(
        block_source.T,
        documents.reshape(-1),
        query_matrix.reshape(*blocks, width),
        key_matrix.reshape(*blocks, kv_width),
        value_matrix.reshape(*blocks, kv_width),
    )
    attended = pl.pallas_call(
        finish_kernel,
        out_shape=jax.ShapeDtypeStruct((*blocks, width), bf16),
        in_specs=[vmem, vmem, vmem, vmem],
        out_specs=anywhere,
        scratch_shapes=[pltpu.VMEM((*blocks, TAIL_WIDTH), bf16), dma((BLK_DEV + 1,))],
        compiler_params=pltpu.CompilerParams(vmem_limit_bytes=16 << 20),
        name="finish_attention",
    )(*parts)
    return attended.reshape(1, BLK_DEV * tokens, width)


def solution(mesh):
    placed = (P("dp", "sp", None), P("dp", "sp", None), P("dp", "sp", None), P(), P("dp", None))
    return jax.shard_map(
        on_device, mesh=mesh, in_specs=placed, out_specs=P("dp", "sp", None), check_vma=False
    )
```

```python
import jax
import jax.numpy as jnp
from jax import lax
from jax.experimental import pallas as pl
from jax.experimental.pallas import tpu as pltpu
from jax.sharding import PartitionSpec as P

QUERY_HEADS = 64
KEY_VALUE_HEADS = 8
HEAD_WIDTH = 128
BALANCE_TOKENS = 128
MOST_BLK = 8
BLK_DEV = 4
N_DP = 4
N_SP = 32
GROUP = QUERY_HEADS // KEY_VALUE_HEADS
PAIR = 2
TWICE = 2
WHOLE = KEY_VALUE_HEADS - 2
HALF = GROUP // 2
LAST = KEY_VALUE_HEADS - 1
PAIRS = GROUP // PAIR - 1
HEAD_GROUPS = WHOLE - TWICE
GROUPS = HEAD_GROUPS + 2 + PAIRS + 1
TAIL = QUERY_HEADS - PAIR
TAIL_WIDTH = PAIR * HEAD_WIDTH
READY_WIDTH = TAIL * HEAD_WIDTH
PIECE_HEADS = (8,)
PIECES = len(PIECE_HEADS)
HALO = MOST_BLK - 1
WINDOW = HALO + BLK_DEV
SPAN = MOST_BLK * BALANCE_TOKENS
MASKED = -1e30
LOG2E = 1.4426950408889634
MESH = pl.DeviceIdType.MESH


def piece_range(piece):
    return sum(PIECE_HEADS[:piece]), PIECE_HEADS[piece]


def causal_levels():
    row = lax.broadcasted_iota(jnp.int32, (BALANCE_TOKENS, BALANCE_TOKENS), 0)
    column = lax.broadcasted_iota(jnp.int32, (BALANCE_TOKENS, BALANCE_TOKENS), 1)
    triangle = jnp.where(column <= row, 0.0, MASKED).astype(jnp.float32)
    return jnp.concatenate([triangle] * PAIR, axis=0)


def attend_pair(queries, keys, values, level, diagonal):
    factor = LOG2E * HEAD_WIDTH ** -0.5
    widened = jnp.concatenate([values, jnp.ones_like(values)], axis=1)
    scores = lax.dot_general(
        queries, keys, (((1,), (1,)), ((), ())), preferred_element_type=jnp.float32
    )
    far = scores[:, : HALO * BALANCE_TOKENS] + level
    near = scores[:, HALO * BALANCE_TOKENS :] + diagonal
    scores = jnp.concatenate([far, near], axis=1)
    top = jnp.max(scores, axis=1, keepdims=True)
    weights = jnp.exp2((scores - top) * factor)
    mixed = jnp.dot(weights.astype(jnp.bfloat16), widened, preferred_element_type=jnp.float32)
    result = (mixed[:, :HEAD_WIDTH] / mixed[:, HEAD_WIDTH:]).astype(jnp.bfloat16)
    return jnp.concatenate(
        [result[h * BALANCE_TOKENS : (h + 1) * BALANCE_TOKENS] for h in range(PAIR)], axis=1
    )


def finish_kernel(ready_ref, queries_ref, window_ref, bias_ref, out_hbm, staged, sem):
    columns = pl.ds(0, READY_WIDTH)
    whole = pltpu.make_async_copy(
        ready_ref.at[:, :, columns], out_hbm.at[:, :, columns], sem.at[0]
    )
    whole.start()
    diagonal = causal_levels()
    for slot in range(BLK_DEV):
        staged[slot] = attend_pair(
            queries_ref[slot],
            window_ref[pl.ds(slot, MOST_BLK), 0].reshape(SPAN, HEAD_WIDTH),
            window_ref[pl.ds(slot, MOST_BLK), 1].reshape(SPAN, HEAD_WIDTH),
            bias_ref[slot, pl.ds(0, 1)],
            diagonal,
        )
    last = pltpu.make_async_copy(
        staged, out_hbm.at[:, :, pl.ds(READY_WIDTH, TAIL_WIDTH)], sem.at[1]
    )
    last.start()
    whole.wait()
    last.wait()


def fused_kernel(
    source_hbm,
    docs_ref,
    q_hbm,
    k_hbm,
    v_hbm,
    out_ref,
    tail_queries,
    tail_window,
    bias,
    source_ref,
    q_local,
    k_local,
    v_local,
    q_send,
    q_recv,
    kv_send,
    kv_recv,
    window,
    load_sem,
    q_load_sem,
    q_send_sem,
    q_recv_sem,
    kv_send_sem,
    kv_recv_sem,
    halo_send_sem,
    halo_recv_sem,
    ready,
):
    g = lax.axis_index("dp")
    s = lax.axis_index("sp")

    def dp_peer(step):
        return (lax.rem(g + step, N_DP), s)

    def sp_peer(step):
        return (g, lax.rem(s + step, N_SP))

    source_load = pltpu.make_async_copy(source_hbm, source_ref, load_sem.at[0])

    def kv_load(kind, piece):
        first, count = piece_range(piece)
        columns = pl.ds(first * HEAD_WIDTH, count * HEAD_WIDTH)
        return pltpu.make_async_copy(
            (k_hbm, v_hbm)[kind].at[:, :, columns],
            (k_local, v_local)[kind][piece],
            load_sem.at[1 + 2 * piece + kind],
        )

    source_load.start()
    for piece in range(PIECES):
        kv_load(0, piece).start()
        kv_load(1, piece).start()

    def q_load(c):
        columns = pl.ds(c * GROUP * HEAD_WIDTH, GROUP * HEAD_WIDTH)
        return pltpu.make_async_copy(
            q_hbm.at[:, :, columns], q_local.at[:, :, columns], q_load_sem.at[c]
        )

    barrier = pltpu.get_barrier_semaphore()
    for step in range(1, N_DP):
        pl.semaphore_signal(barrier, 1, device_id=dp_peer(step), device_id_type=MESH)

    def greet(semaphore, column):
        pl.semaphore_signal(semaphore, 1, device_id=(g, column), device_id_type=MESH)

    @pl.when((s == 1) | (s >= 3))
    def _():
        greet(barrier, s - 1)

    @pl.when(s >= 4)
    def _():
        greet(barrier, s - 2)

    def enter():
        @pl.when(s == 0)
        def _():
            pl.semaphore_wait(barrier, 4)
            greet(barrier, 2)

        @pl.when(s == 1)
        def _():
            pl.semaphore_wait(barrier, 3)
            greet(barrier, 2)
            greet(barrier, 3)

        @pl.when(s == 2)
        def _():
            pl.semaphore_wait(barrier, 7)
            greet(ready, 0)
            greet(ready, 1)

        @pl.when(s == 3)
        def _():
            pl.semaphore_wait(barrier, 6)
            greet(ready, 1)

        @pl.when((s >= 4) & (s <= N_SP - 3))
        def _():
            pl.semaphore_wait(barrier, 5)

        @pl.when(s == N_SP - 2)
        def _():
            pl.semaphore_wait(barrier, 4)

        @pl.when(s == N_SP - 1)
        def _():
            pl.semaphore_wait(barrier, 3)

    source_load.wait()

    def departing(step):
        dest = lax.rem(g + step, N_DP)
        chosen = 0
        for slot in range(BLK_DEV):
            entry = source_ref[dest * BLK_DEV + slot, s]
            chosen = chosen + jnp.where((entry >> 2) == g, entry & 3, 0)
        return chosen

    def arrived_from(slot):
        entry = source_ref[g * BLK_DEV + slot, s]
        return (g - (entry >> 2)) & 3

    leaves = [departing(step) for step in range(N_DP)]
    comes = [arrived_from(slot) for slot in range(BLK_DEV)]

    def turns(turn, number):
        if turn >= 2:
            step = (2, 0)[turn - 2]
            return step, leaves[step]
        step = 1 + 2 * lax.rem(s + number + turn, 2)
        return step, jnp.where(step == 1, leaves[1], leaves[3])

    def kv_copy(piece, step):
        heads = pl.ds(*piece_range(piece))
        return pltpu.make_async_remote_copy(
            src_ref=kv_send.at[step - 1, heads],
            dst_ref=kv_recv.at[step, heads],
            send_sem=kv_send_sem.at[piece, step - 1],
            recv_sem=kv_recv_sem.at[piece, step - 1],
            device_id=dp_peer(step),
            device_id_type=MESH,
        )

    def q_copy(group, first, count, step):
        heads = pl.ds(first, count)
        return pltpu.make_async_remote_copy(
            src_ref=q_send.at[step - 1, heads],
            dst_ref=q_recv.at[step, heads],
            send_sem=q_send_sem.at[group, step - 1],
            recv_sem=q_recv_sem.at[group, step - 1],
            device_id=dp_peer(step),
            device_id_type=MESH,
        )

    def each_group(act):
        @pl.loop(0, TWICE)
        def _(i):
            act(i, i * 2 * GROUP, 2 * GROUP)

        @pl.loop(2 * TWICE, WHOLE)
        def _(c):
            act(c - TWICE, c * GROUP, GROUP)

        @pl.loop(0, 2)
        def _(i):
            act(HEAD_GROUPS + i, WHOLE * GROUP + i * HALF, HALF)

        @pl.loop(0, PAIRS + 1)
        def _(i):
            act(HEAD_GROUPS + 2 + i, LAST * GROUP + i * PAIR, PAIR)


    def near_copy(c):
        return pltpu.make_async_remote_copy(
            src_ref=window.at[c, pl.ds(HALO, BLK_DEV)],
            dst_ref=window.at[c, pl.ds(HALO - BLK_DEV, BLK_DEV)],
            send_sem=halo_send_sem.at[c, 0],
            recv_sem=halo_recv_sem.at[c, 0],
            device_id=sp_peer(1),
            device_id_type=MESH,
        )

    def far_copy(c):
        return pltpu.make_async_remote_copy(
            src_ref=window.at[c, pl.ds(WINDOW - (HALO - BLK_DEV), HALO - BLK_DEV)],
            dst_ref=window.at[c, pl.ds(0, HALO - BLK_DEV)],
            send_sem=halo_send_sem.at[c, 1],
            recv_sem=halo_recv_sem.at[c, 1],
            device_id=sp_peer(2),
            device_id_type=MESH,
        )

    for piece in range(PIECES):
        kv_load(0, piece).wait()
        kv_load(1, piece).wait()
        if piece == PIECES - 1:
            for c in range(KEY_VALUE_HEADS):
                q_load(c).start()
        for turn in range(N_DP):
            step, leaf = turns(turn, piece)
            first, count = piece_range(piece)
            for head in range(count):
                columns = pl.ds(head * HEAD_WIDTH, HEAD_WIDTH)
                key = k_local[piece][leaf, :, columns]
                value = v_local[piece][leaf, :, columns]
                if turn < N_DP - 1:
                    kv_send[step - 1, first + head, 0] = key
                    kv_send[step - 1, first + head, 1] = value
                else:
                    kv_recv[0, first + head, 0] = key
                    kv_recv[0, first + head, 1] = value
            if piece == 0 and turn == 0:
                enter()
            if turn < N_DP - 1:
                kv_copy(piece, step).start()

    for c in range(KEY_VALUE_HEADS):
        q_load(c).wait()

    def send_group(group, first, count):
        for turn in range(N_DP):
            step, leaf = turns(turn, group)
            for i in range(count):
                head = first + i
                columns = pl.ds(pl.multiple_of(head * HEAD_WIDTH, HEAD_WIDTH), HEAD_WIDTH)
                block = q_local[leaf, :, columns]
                if turn < N_DP - 1:
                    q_send[step - 1, head] = block
                else:
                    q_recv[0, head] = block
            if turn < N_DP - 1:
                q_copy(group, first, count, step).start()

    each_group(send_group)

    for slot in range(BLK_DEV):
        own = docs_ref[s * BLK_DEV + slot]
        for j in range(HALO):
            block = s * BLK_DEV + slot + j - HALO
            same = (docs_ref[jnp.maximum(block, 0)] == own) & (block >= 0)
            level = jnp.where(same, 0.0, MASKED).astype(jnp.float32)
            bias[slot, :, pl.ds(j * BALANCE_TOKENS, BALANCE_TOKENS)] = jnp.full(
                (8, BALANCE_TOKENS), level, jnp.float32
            )

    for piece in range(PIECES):
        for step in range(1, N_DP):
            kv_copy(piece, step).wait_recv()
    for slot in range(BLK_DEV):
        for c in range(KEY_VALUE_HEADS):
            window[c, HALO + slot] = kv_recv[comes[slot], c]

    def each_halo(near_act, far_act, near_when, far_when):
        @pl.when(near_when)
        def _():
            @pl.loop(0, KEY_VALUE_HEADS)
            def _(c):
                near_act(c)

                @pl.when(far_when)
                def _():
                    far_act(c)

    @pl.when(s == 0)
    def _():
        pl.semaphore_wait(ready, 1)

    @pl.when(s == 1)
    def _():
        pl.semaphore_wait(ready, 2)

    each_halo(
        lambda c: near_copy(c).start(),
        lambda c: far_copy(c).start(),
        s < N_SP - 1,
        s < N_SP - 2,
    )

    @pl.when(s < 2)
    def _():
        @pl.loop(0, KEY_VALUE_HEADS)
        def _(c):
            window[c, pl.ds(0, HALO - BLK_DEV)] = jnp.zeros(
                (HALO - BLK_DEV, 2, BALANCE_TOKENS, HEAD_WIDTH), jnp.bfloat16
            )

    @pl.when(s < 1)
    def _():
        @pl.loop(0, KEY_VALUE_HEADS)
        def _(c):
            window[c, pl.ds(HALO - BLK_DEV, BLK_DEV)] = jnp.zeros(
                (BLK_DEV, 2, BALANCE_TOKENS, HEAD_WIDTH), jnp.bfloat16
            )

    def slot_queries(slot, first, count):
        heads = pl.ds(first, count)
        arrived = q_recv[0, heads]
        for step in range(1, N_DP):
            arrived = jnp.where(comes[slot] == step, q_recv[step, heads], arrived)
        return arrived.reshape(count * BALANCE_TOKENS, HEAD_WIDTH)

    diagonal = causal_levels()

    def attend(c, first):
        for slot in range(BLK_DEV):
            columns = pl.ds(pl.multiple_of(first * HEAD_WIDTH, TAIL_WIDTH), TAIL_WIDTH)
            out_ref[slot, :, columns] = attend_pair(
                slot_queries(slot, first, PAIR),
                window[c, pl.ds(slot, MOST_BLK), 0].reshape(SPAN, HEAD_WIDTH),
                window[c, pl.ds(slot, MOST_BLK), 1].reshape(SPAN, HEAD_WIDTH),
                bias[slot, pl.ds(0, 1)],
                diagonal,
            )

    def await_group(group, first, count):
        for step in range(1, N_DP):
            q_copy(group, first, count, step).wait_recv()

    def sent_group(group, first, count):
        for step in range(1, N_DP):
            q_copy(group, first, count, step).wait_send()

    def await_halo(c):
        @pl.when(s >= 1)
        def _():
            near_copy(c).wait_recv()

        @pl.when(s >= 2)
        def _():
            far_copy(c).wait_recv()

    def attend_whole(c):
        await_halo(c)

        @pl.loop(0, GROUP // PAIR)
        def _(i):
            attend(c, c * GROUP + i * PAIR)

    @pl.loop(0, TWICE)
    def _(i):
        await_group(i, i * 2 * GROUP, 2 * GROUP)

        @pl.loop(0, 2)
        def _(j):
            attend_whole(2 * i + j)

    @pl.loop(2 * TWICE, WHOLE)
    def _(c):
        await_group(c - TWICE, c * GROUP, GROUP)
        attend_whole(c)

    await_halo(WHOLE)

    @pl.loop(0, 2)
    def _(i):
        await_group(HEAD_GROUPS + i, WHOLE * GROUP + i * HALF, HALF)

        @pl.loop(0, HALF // PAIR)
        def _(j):
            attend(WHOLE, WHOLE * GROUP + i * HALF + j * PAIR)

    await_halo(LAST)
    tail_window[...] = window[LAST]
    for piece in range(PIECES):
        for step in range(1, N_DP):
            kv_copy(piece, step).wait_send()

    each_halo(
        lambda c: near_copy(c).wait_send(),
        lambda c: far_copy(c).wait_send(),
        s < N_SP - 1,
        s < N_SP - 2,
    )

    @pl.loop(0, TWICE)
    def _(i):
        sent_group(i, i * 2 * GROUP, 2 * GROUP)

    @pl.loop(2 * TWICE, WHOLE)
    def _(c):
        sent_group(c - TWICE, c * GROUP, GROUP)

    @pl.loop(0, 2)
    def _(i):
        sent_group(HEAD_GROUPS + i, WHOLE * GROUP + i * HALF, HALF)

    @pl.loop(0, PAIRS)
    def _(i):
        await_group(HEAD_GROUPS + 2 + i, LAST * GROUP + i * PAIR, PAIR)
        attend(LAST, LAST * GROUP + i * PAIR)
        sent_group(HEAD_GROUPS + 2 + i, LAST * GROUP + i * PAIR, PAIR)

    await_group(GROUPS - 1, TAIL, PAIR)
    for slot in range(BLK_DEV):
        tail_queries[slot] = slot_queries(slot, TAIL, PAIR)
    sent_group(GROUPS - 1, TAIL, PAIR)


def on_device(query_matrix, key_matrix, value_matrix, block_source, documents):
    bf16 = jnp.bfloat16
    tokens = BALANCE_TOKENS
    blocks = (BLK_DEV, tokens)
    dma = pltpu.SemaphoreType.DMA
    kv_width = KEY_VALUE_HEADS * HEAD_WIDTH
    width = QUERY_HEADS * HEAD_WIDTH
    smem = pl.BlockSpec(memory_space=pltpu.SMEM)
    anywhere = pl.BlockSpec(memory_space=pl.ANY)
    vmem = pl.BlockSpec(memory_space=pltpu.VMEM)
    parts = pl.pallas_call(
        fused_kernel,
        out_shape=(
            pltpu.VMEM((*blocks, width), bf16),
            pltpu.VMEM((BLK_DEV, PAIR * tokens, HEAD_WIDTH), bf16),
            pltpu.VMEM((WINDOW, 2, tokens, HEAD_WIDTH), bf16),
            pltpu.VMEM((BLK_DEV, 8, HALO * tokens), jnp.float32),
        ),
        in_specs=[anywhere, smem, anywhere, anywhere, anywhere],
        out_specs=(vmem, vmem, vmem, vmem),
        scratch_shapes=[
            pltpu.SMEM(block_source.shape[::-1], jnp.int32),
            pltpu.VMEM((*blocks, width), bf16),
            [pltpu.VMEM((*blocks, count * HEAD_WIDTH), bf16) for count in PIECE_HEADS],
            [pltpu.VMEM((*blocks, count * HEAD_WIDTH), bf16) for count in PIECE_HEADS],
            pltpu.VMEM((N_DP - 1, QUERY_HEADS, tokens, HEAD_WIDTH), bf16),
            pltpu.VMEM((N_DP, QUERY_HEADS, tokens, HEAD_WIDTH), bf16),
            pltpu.VMEM((N_DP - 1, KEY_VALUE_HEADS, 2, tokens, HEAD_WIDTH), bf16),
            pltpu.VMEM((N_DP, KEY_VALUE_HEADS, 2, tokens, HEAD_WIDTH), bf16),
            pltpu.VMEM((KEY_VALUE_HEADS, WINDOW, 2, tokens, HEAD_WIDTH), bf16),
            dma((1 + 2 * PIECES,)),
            dma((KEY_VALUE_HEADS,)),
            dma((GROUPS, N_DP - 1)),
            dma((GROUPS, N_DP - 1)),
            dma((PIECES, N_DP - 1)),
            dma((PIECES, N_DP - 1)),
            dma((KEY_VALUE_HEADS, 2)),
            dma((KEY_VALUE_HEADS, 2)),
            pltpu.SemaphoreType.REGULAR,
        ],
        compiler_params=pltpu.CompilerParams(
            collective_id=0, has_side_effects=True, vmem_limit_bytes=48 << 20
        ),
        name="balanced_attention",
    )(
        block_source.T,
        documents.reshape(-1),
        query_matrix.reshape(*blocks, width),
        key_matrix.reshape(*blocks, kv_width),
        value_matrix.reshape(*blocks, kv_width),
    )
    attended = pl.pallas_call(
        finish_kernel,
        out_shape=jax.ShapeDtypeStruct((*blocks, width), bf16),
        in_specs=[vmem, vmem, vmem, vmem],
        out_specs=anywhere,
        scratch_shapes=[pltpu.VMEM((*blocks, TAIL_WIDTH), bf16), dma((2,))],
        compiler_params=pltpu.CompilerParams(vmem_limit_bytes=16 << 20),
        name="finish_attention",
    )(*parts)
    return attended.reshape(1, BLK_DEV * tokens, width)


def solution(mesh):
    placed = (P("dp", "sp", None), P("dp", "sp", None), P("dp", "sp", None), P(), P("dp", None))
    return jax.shard_map(
        on_device, mesh=mesh, in_specs=placed, out_specs=P("dp", "sp", None), check_vma=False
    )
```

```python
import jax
import jax.numpy as jnp
from jax import lax
from jax.experimental import pallas as pl
from jax.experimental.pallas import tpu as pltpu
from jax.sharding import PartitionSpec as P

QUERY_HEADS = 64
KEY_VALUE_HEADS = 8
HEAD_WIDTH = 128
BALANCE_TOKENS = 128
MOST_BLK = 8
BLK_DEV = 4
N_DP = 4
N_SP = 32
GROUP = QUERY_HEADS // KEY_VALUE_HEADS
PAIR = 2
TWICE = 2
WHOLE = KEY_VALUE_HEADS - 2
HALF = GROUP // 2
LAST = KEY_VALUE_HEADS - 1
PAIRS = GROUP // PAIR - 1
HEAD_GROUPS = WHOLE - TWICE
GROUPS = HEAD_GROUPS + 2 + PAIRS + 1
TAIL = QUERY_HEADS - PAIR
TAIL_WIDTH = PAIR * HEAD_WIDTH
READY_WIDTH = TAIL * HEAD_WIDTH
PIECE_HEADS = (8,)
PIECES = len(PIECE_HEADS)
HALO = MOST_BLK - 1
WINDOW = HALO + BLK_DEV
SPAN = MOST_BLK * BALANCE_TOKENS
MASKED = -1e30
LOG2E = 1.4426950408889634
MESH = pl.DeviceIdType.MESH


def piece_range(piece):
    return sum(PIECE_HEADS[:piece]), PIECE_HEADS[piece]


def causal_levels():
    row = lax.broadcasted_iota(jnp.int32, (BALANCE_TOKENS, BALANCE_TOKENS), 0)
    column = lax.broadcasted_iota(jnp.int32, (BALANCE_TOKENS, BALANCE_TOKENS), 1)
    triangle = jnp.where(column <= row, 0.0, MASKED).astype(jnp.float32)
    return jnp.concatenate([triangle] * PAIR, axis=0)


def attend_pair(queries, keys, values, level, diagonal):
    factor = LOG2E * HEAD_WIDTH ** -0.5
    widened = jnp.concatenate([values, jnp.ones_like(values)], axis=1)
    scores = lax.dot_general(
        queries, keys, (((1,), (1,)), ((), ())), preferred_element_type=jnp.float32
    )
    far = scores[:, : HALO * BALANCE_TOKENS] + level
    near = scores[:, HALO * BALANCE_TOKENS :] + diagonal
    scores = jnp.concatenate([far, near], axis=1)
    top = jnp.max(scores, axis=1, keepdims=True)
    weights = jnp.exp2((scores - top) * factor)
    mixed = jnp.dot(weights.astype(jnp.bfloat16), widened, preferred_element_type=jnp.float32)
    result = (mixed[:, :HEAD_WIDTH] / mixed[:, HEAD_WIDTH:]).astype(jnp.bfloat16)
    return jnp.concatenate(
        [result[h * BALANCE_TOKENS : (h + 1) * BALANCE_TOKENS] for h in range(PAIR)], axis=1
    )


def finish_kernel(ready_ref, queries_ref, window_ref, bias_ref, out_hbm, staged, sem):
    columns = pl.ds(0, READY_WIDTH)
    whole = pltpu.make_async_copy(
        ready_ref.at[:, :, columns], out_hbm.at[:, :, columns], sem.at[0]
    )
    whole.start()
    diagonal = causal_levels()
    for slot in range(BLK_DEV):
        staged[slot] = attend_pair(
            queries_ref[slot],
            window_ref[pl.ds(slot, MOST_BLK), 0].reshape(SPAN, HEAD_WIDTH),
            window_ref[pl.ds(slot, MOST_BLK), 1].reshape(SPAN, HEAD_WIDTH),
            bias_ref[slot, pl.ds(0, 1)],
            diagonal,
        )
    last = pltpu.make_async_copy(
        staged, out_hbm.at[:, :, pl.ds(READY_WIDTH, TAIL_WIDTH)], sem.at[1]
    )
    last.start()
    whole.wait()
    last.wait()


def fused_kernel(
    source_hbm,
    docs_ref,
    q_hbm,
    k_hbm,
    v_hbm,
    out_ref,
    tail_queries,
    tail_window,
    bias,
    source_ref,
    q_local,
    k_local,
    v_local,
    q_send,
    q_recv,
    kv_send,
    kv_recv,
    window,
    load_sem,
    q_load_sem,
    q_send_sem,
    q_recv_sem,
    kv_send_sem,
    kv_recv_sem,
    halo_send_sem,
    halo_recv_sem,
    ready,
):
    g = lax.axis_index("dp")
    s = lax.axis_index("sp")

    def dp_peer(step):
        return (lax.rem(g + step, N_DP), s)

    def sp_peer(step):
        return (g, lax.rem(s + step, N_SP))

    source_load = pltpu.make_async_copy(source_hbm, source_ref, load_sem.at[0])

    def kv_load(kind, piece):
        first, count = piece_range(piece)
        columns = pl.ds(first * HEAD_WIDTH, count * HEAD_WIDTH)
        return pltpu.make_async_copy(
            (k_hbm, v_hbm)[kind].at[:, :, columns],
            (k_local, v_local)[kind][piece],
            load_sem.at[1 + 2 * piece + kind],
        )


    def q_load(c):
        columns = pl.ds(c * GROUP * HEAD_WIDTH, GROUP * HEAD_WIDTH)
        return pltpu.make_async_copy(
            q_hbm.at[:, :, columns], q_local.at[:, :, columns], q_load_sem.at[c]
        )

    barrier = pltpu.get_barrier_semaphore()
    for step in range(1, N_DP):
        pl.semaphore_signal(barrier, 1, device_id=dp_peer(step), device_id_type=MESH)

    def greet(semaphore, column):
        pl.semaphore_signal(semaphore, 1, device_id=(g, column), device_id_type=MESH)

    @pl.when((s == 1) | (s >= 3))
    def _():
        greet(barrier, s - 1)

    @pl.when(s >= 4)
    def _():
        greet(barrier, s - 2)

    def enter():
        @pl.when(s == 0)
        def _():
            pl.semaphore_wait(barrier, 4)
            greet(barrier, 2)

        @pl.when(s == 1)
        def _():
            pl.semaphore_wait(barrier, 3)
            greet(barrier, 2)
            greet(barrier, 3)

        @pl.when(s == 2)
        def _():
            pl.semaphore_wait(barrier, 7)
            greet(ready, 0)
            greet(ready, 1)

        @pl.when(s == 3)
        def _():
            pl.semaphore_wait(barrier, 6)
            greet(ready, 1)

        @pl.when((s >= 4) & (s <= N_SP - 3))
        def _():
            pl.semaphore_wait(barrier, 5)

        @pl.when(s == N_SP - 2)
        def _():
            pl.semaphore_wait(barrier, 4)

        @pl.when(s == N_SP - 1)
        def _():
            pl.semaphore_wait(barrier, 3)

    source_load.start()
    for piece in range(PIECES):
        kv_load(0, piece).start()
        kv_load(1, piece).start()
    source_load.wait()

    def departing(step):
        dest = lax.rem(g + step, N_DP)
        chosen = 0
        for slot in range(BLK_DEV):
            entry = source_ref[dest * BLK_DEV + slot, s]
            chosen = chosen + jnp.where((entry >> 2) == g, entry & 3, 0)
        return chosen

    def arrived_from(slot):
        entry = source_ref[g * BLK_DEV + slot, s]
        return (g - (entry >> 2)) & 3

    leaves = [departing(step) for step in range(N_DP)]
    comes = [arrived_from(slot) for slot in range(BLK_DEV)]

    def turns(turn, number):
        if turn >= 2:
            step = (2, 0)[turn - 2]
            return step, leaves[step]
        step = 1 + 2 * lax.rem(s + number + turn, 2)
        return step, jnp.where(step == 1, leaves[1], leaves[3])

    def kv_copy(piece, step):
        heads = pl.ds(*piece_range(piece))
        return pltpu.make_async_remote_copy(
            src_ref=kv_send.at[step - 1, heads],
            dst_ref=kv_recv.at[step, heads],
            send_sem=kv_send_sem.at[piece, step - 1],
            recv_sem=kv_recv_sem.at[piece, step - 1],
            device_id=dp_peer(step),
            device_id_type=MESH,
        )

    def q_copy(group, first, count, step):
        heads = pl.ds(first, count)
        return pltpu.make_async_remote_copy(
            src_ref=q_send.at[step - 1, heads],
            dst_ref=q_recv.at[step, heads],
            send_sem=q_send_sem.at[group, step - 1],
            recv_sem=q_recv_sem.at[group, step - 1],
            device_id=dp_peer(step),
            device_id_type=MESH,
        )

    def each_group(act):
        @pl.loop(0, TWICE)
        def _(i):
            act(i, i * 2 * GROUP, 2 * GROUP)

        @pl.loop(2 * TWICE, WHOLE)
        def _(c):
            act(c - TWICE, c * GROUP, GROUP)

        @pl.loop(0, 2)
        def _(i):
            act(HEAD_GROUPS + i, WHOLE * GROUP + i * HALF, HALF)

        @pl.loop(0, PAIRS + 1)
        def _(i):
            act(HEAD_GROUPS + 2 + i, LAST * GROUP + i * PAIR, PAIR)


    def near_copy(c):
        return pltpu.make_async_remote_copy(
            src_ref=window.at[c, pl.ds(HALO, BLK_DEV)],
            dst_ref=window.at[c, pl.ds(HALO - BLK_DEV, BLK_DEV)],
            send_sem=halo_send_sem.at[c, 0],
            recv_sem=halo_recv_sem.at[c, 0],
            device_id=sp_peer(1),
            device_id_type=MESH,
        )

    def far_copy(c):
        return pltpu.make_async_remote_copy(
            src_ref=window.at[c, pl.ds(WINDOW - (HALO - BLK_DEV), HALO - BLK_DEV)],
            dst_ref=window.at[c, pl.ds(0, HALO - BLK_DEV)],
            send_sem=halo_send_sem.at[c, 1],
            recv_sem=halo_recv_sem.at[c, 1],
            device_id=sp_peer(2),
            device_id_type=MESH,
        )

    for piece in range(PIECES):
        kv_load(0, piece).wait()
        kv_load(1, piece).wait()
        if piece == PIECES - 1:
            for c in range(KEY_VALUE_HEADS):
                q_load(c).start()
        for turn in range(N_DP):
            step, leaf = turns(turn, piece)
            first, count = piece_range(piece)
            for head in range(count):
                columns = pl.ds(head * HEAD_WIDTH, HEAD_WIDTH)
                key = k_local[piece][leaf, :, columns]
                value = v_local[piece][leaf, :, columns]
                if turn < N_DP - 1:
                    kv_send[step - 1, first + head, 0] = key
                    kv_send[step - 1, first + head, 1] = value
                else:
                    kv_recv[0, first + head, 0] = key
                    kv_recv[0, first + head, 1] = value
            if piece == 0 and turn == 0:
                enter()
            if turn < N_DP - 1:
                kv_copy(piece, step).start()

    for c in range(KEY_VALUE_HEADS):
        q_load(c).wait()

    def send_group(group, first, count):
        for turn in range(N_DP):
            step, leaf = turns(turn, group)
            for i in range(count):
                head = first + i
                columns = pl.ds(pl.multiple_of(head * HEAD_WIDTH, HEAD_WIDTH), HEAD_WIDTH)
                block = q_local[leaf, :, columns]
                if turn < N_DP - 1:
                    q_send[step - 1, head] = block
                else:
                    q_recv[0, head] = block
            if turn < N_DP - 1:
                q_copy(group, first, count, step).start()

    each_group(send_group)

    for slot in range(BLK_DEV):
        own = docs_ref[s * BLK_DEV + slot]
        for j in range(HALO):
            block = s * BLK_DEV + slot + j - HALO
            same = (docs_ref[jnp.maximum(block, 0)] == own) & (block >= 0)
            level = jnp.where(same, 0.0, MASKED).astype(jnp.float32)
            bias[slot, :, pl.ds(j * BALANCE_TOKENS, BALANCE_TOKENS)] = jnp.full(
                (8, BALANCE_TOKENS), level, jnp.float32
            )

    for piece in range(PIECES):
        for step in range(1, N_DP):
            kv_copy(piece, step).wait_recv()
    for slot in range(BLK_DEV):
        for c in range(KEY_VALUE_HEADS):
            window[c, HALO + slot] = kv_recv[comes[slot], c]

    def each_halo(near_act, far_act, near_when, far_when):
        @pl.when(near_when)
        def _():
            @pl.loop(0, KEY_VALUE_HEADS)
            def _(c):
                near_act(c)

                @pl.when(far_when)
                def _():
                    far_act(c)

    @pl.when(s == 0)
    def _():
        pl.semaphore_wait(ready, 1)

    @pl.when(s == 1)
    def _():
        pl.semaphore_wait(ready, 2)

    each_halo(
        lambda c: near_copy(c).start(),
        lambda c: far_copy(c).start(),
        s < N_SP - 1,
        s < N_SP - 2,
    )

    @pl.when(s < 2)
    def _():
        @pl.loop(0, KEY_VALUE_HEADS)
        def _(c):
            window[c, pl.ds(0, HALO - BLK_DEV)] = jnp.zeros(
                (HALO - BLK_DEV, 2, BALANCE_TOKENS, HEAD_WIDTH), jnp.bfloat16
            )

    @pl.when(s < 1)
    def _():
        @pl.loop(0, KEY_VALUE_HEADS)
        def _(c):
            window[c, pl.ds(HALO - BLK_DEV, BLK_DEV)] = jnp.zeros(
                (BLK_DEV, 2, BALANCE_TOKENS, HEAD_WIDTH), jnp.bfloat16
            )

    def slot_queries(slot, first, count):
        heads = pl.ds(first, count)
        arrived = q_recv[0, heads]
        for step in range(1, N_DP):
            arrived = jnp.where(comes[slot] == step, q_recv[step, heads], arrived)
        return arrived.reshape(count * BALANCE_TOKENS, HEAD_WIDTH)

    diagonal = causal_levels()

    def attend(c, first):
        for slot in range(BLK_DEV):
            columns = pl.ds(pl.multiple_of(first * HEAD_WIDTH, TAIL_WIDTH), TAIL_WIDTH)
            out_ref[slot, :, columns] = attend_pair(
                slot_queries(slot, first, PAIR),
                window[c, pl.ds(slot, MOST_BLK), 0].reshape(SPAN, HEAD_WIDTH),
                window[c, pl.ds(slot, MOST_BLK), 1].reshape(SPAN, HEAD_WIDTH),
                bias[slot, pl.ds(0, 1)],
                diagonal,
            )

    def await_group(group, first, count):
        for step in range(1, N_DP):
            q_copy(group, first, count, step).wait_recv()

    def sent_group(group, first, count):
        for step in range(1, N_DP):
            q_copy(group, first, count, step).wait_send()

    def await_halo(c):
        @pl.when(s >= 1)
        def _():
            near_copy(c).wait_recv()

        @pl.when(s >= 2)
        def _():
            far_copy(c).wait_recv()

    def attend_whole(c):
        await_halo(c)

        @pl.loop(0, GROUP // PAIR)
        def _(i):
            attend(c, c * GROUP + i * PAIR)

    @pl.loop(0, TWICE)
    def _(i):
        await_group(i, i * 2 * GROUP, 2 * GROUP)

        @pl.loop(0, 2)
        def _(j):
            attend_whole(2 * i + j)

    @pl.loop(2 * TWICE, WHOLE)
    def _(c):
        await_group(c - TWICE, c * GROUP, GROUP)
        attend_whole(c)

    await_halo(WHOLE)

    @pl.loop(0, 2)
    def _(i):
        await_group(HEAD_GROUPS + i, WHOLE * GROUP + i * HALF, HALF)

        @pl.loop(0, HALF // PAIR)
        def _(j):
            attend(WHOLE, WHOLE * GROUP + i * HALF + j * PAIR)

    await_halo(LAST)
    tail_window[...] = window[LAST]
    for piece in range(PIECES):
        for step in range(1, N_DP):
            kv_copy(piece, step).wait_send()

    each_halo(
        lambda c: near_copy(c).wait_send(),
        lambda c: far_copy(c).wait_send(),
        s < N_SP - 1,
        s < N_SP - 2,
    )

    @pl.loop(0, TWICE)
    def _(i):
        sent_group(i, i * 2 * GROUP, 2 * GROUP)

    @pl.loop(2 * TWICE, WHOLE)
    def _(c):
        sent_group(c - TWICE, c * GROUP, GROUP)

    @pl.loop(0, 2)
    def _(i):
        sent_group(HEAD_GROUPS + i, WHOLE * GROUP + i * HALF, HALF)

    @pl.loop(0, PAIRS)
    def _(i):
        await_group(HEAD_GROUPS + 2 + i, LAST * GROUP + i * PAIR, PAIR)
        attend(LAST, LAST * GROUP + i * PAIR)
        sent_group(HEAD_GROUPS + 2 + i, LAST * GROUP + i * PAIR, PAIR)

    await_group(GROUPS - 1, TAIL, PAIR)
    for slot in range(BLK_DEV):
        tail_queries[slot] = slot_queries(slot, TAIL, PAIR)
    sent_group(GROUPS - 1, TAIL, PAIR)


def on_device(query_matrix, key_matrix, value_matrix, block_source, documents):
    bf16 = jnp.bfloat16
    tokens = BALANCE_TOKENS
    blocks = (BLK_DEV, tokens)
    dma = pltpu.SemaphoreType.DMA
    kv_width = KEY_VALUE_HEADS * HEAD_WIDTH
    width = QUERY_HEADS * HEAD_WIDTH
    smem = pl.BlockSpec(memory_space=pltpu.SMEM)
    anywhere = pl.BlockSpec(memory_space=pl.ANY)
    vmem = pl.BlockSpec(memory_space=pltpu.VMEM)
    parts = pl.pallas_call(
        fused_kernel,
        out_shape=(
            pltpu.VMEM((*blocks, width), bf16),
            pltpu.VMEM((BLK_DEV, PAIR * tokens, HEAD_WIDTH), bf16),
            pltpu.VMEM((WINDOW, 2, tokens, HEAD_WIDTH), bf16),
            pltpu.VMEM((BLK_DEV, 8, HALO * tokens), jnp.float32),
        ),
        in_specs=[anywhere, smem, anywhere, anywhere, anywhere],
        out_specs=(vmem, vmem, vmem, vmem),
        scratch_shapes=[
            pltpu.SMEM(block_source.shape[::-1], jnp.int32),
            pltpu.VMEM((*blocks, width), bf16),
            [pltpu.VMEM((*blocks, count * HEAD_WIDTH), bf16) for count in PIECE_HEADS],
            [pltpu.VMEM((*blocks, count * HEAD_WIDTH), bf16) for count in PIECE_HEADS],
            pltpu.VMEM((N_DP - 1, QUERY_HEADS, tokens, HEAD_WIDTH), bf16),
            pltpu.VMEM((N_DP, QUERY_HEADS, tokens, HEAD_WIDTH), bf16),
            pltpu.VMEM((N_DP - 1, KEY_VALUE_HEADS, 2, tokens, HEAD_WIDTH), bf16),
            pltpu.VMEM((N_DP, KEY_VALUE_HEADS, 2, tokens, HEAD_WIDTH), bf16),
            pltpu.VMEM((KEY_VALUE_HEADS, WINDOW, 2, tokens, HEAD_WIDTH), bf16),
            dma((1 + 2 * PIECES,)),
            dma((KEY_VALUE_HEADS,)),
            dma((GROUPS, N_DP - 1)),
            dma((GROUPS, N_DP - 1)),
            dma((PIECES, N_DP - 1)),
            dma((PIECES, N_DP - 1)),
            dma((KEY_VALUE_HEADS, 2)),
            dma((KEY_VALUE_HEADS, 2)),
            pltpu.SemaphoreType.REGULAR,
        ],
        compiler_params=pltpu.CompilerParams(
            collective_id=0, has_side_effects=True, vmem_limit_bytes=48 << 20
        ),
        name="balanced_attention",
    )(
        block_source.T,
        documents.reshape(-1),
        query_matrix.reshape(*blocks, width),
        key_matrix.reshape(*blocks, kv_width),
        value_matrix.reshape(*blocks, kv_width),
    )
    attended = pl.pallas_call(
        finish_kernel,
        out_shape=jax.ShapeDtypeStruct((*blocks, width), bf16),
        in_specs=[vmem, vmem, vmem, vmem],
        out_specs=anywhere,
        scratch_shapes=[pltpu.VMEM((*blocks, TAIL_WIDTH), bf16), dma((2,))],
        compiler_params=pltpu.CompilerParams(vmem_limit_bytes=16 << 20),
        name="finish_attention",
    )(*parts)
    return attended.reshape(1, BLK_DEV * tokens, width)


def solution(mesh):
    placed = (P("dp", "sp", None), P("dp", "sp", None), P("dp", "sp", None), P(), P("dp", None))
    return jax.shard_map(
        on_device, mesh=mesh, in_specs=placed, out_specs=P("dp", "sp", None), check_vma=False
    )
```
